1024 devices in a mesh: elem: 64 (over y, z_hi, core), plane: 16 (over z_lo, x).
Axes of the slice: x: 8, y: 8, z: 8 (z_hi: 4, z_lo: 2; z = z_hi * 2 + z_lo), core: 2. Of those that a mesh axis runs over, the one named last changes fastest.
Arguments:
- velocity_modes: bfloat16 [3, 512, 512, 144], P(None, 'plane', 'elem'), may hold values from -0.8 to 0.8
- metric: float32 [512, 4], P('elem'), may hold values from 0.5 to 2
- face_partner: int32 [512, 4], P('elem'), may hold values from -1 to 511, as said below
- face_side: int32 [512, 4], P('elem'), may hold values from 0 to 3
- face_flip: int32 [512, 4], P('elem'), may hold values from 0 to 1
Outputs:
- nonlinear_term: bfloat16 [3, 512, 512, 144], P(None, 'plane', 'elem')
The draws below stay inside these ranges and needn't reach their ends.
Inputs may be any that keep to these rules, and one draw needn't show every extreme that they name: `face_partner`: the faces are mutual: if face f of element e names p with side s and flip t, face s of p names e with side f and flip t. Every partner lies on the same index of elem or on the one before or after it, cyclically; on each index exactly 2 elements have a face whose partner lies on the index before, and exactly 2 on the index after.
All inputs are finite; a program needn't handle non-finite values.
Results may differ from the reference program's by a relative error of at most 0.0076.
Values may be sent and summed in bfloat16 or wider, within the bound.
No kernel may reach another device: no remote copies, remote signals or barrier semaphores. Data moves between devices by JAX's collectives and lax.ppermute only.
A program may use at most 32 MiB of HBM per device.

```python
import math
import jax
import jax.numpy as jnp
import numpy as np
from jax import lax

NPTS = 144
PLANES = 512
E_DEV = 8
EW = 2
ELEMS = 512
PHYS = 768


def face_tables(key):
    blocks = ELEMS // E_DEV
    columns = ELEMS // EW
    block_keys = jax.random.split(jax.random.fold_in(key, 7), blocks)
    shuffled = jax.vmap(lambda sub: jax.random.permutation(sub, E_DEV))(block_keys)
    slot_of = (jnp.arange(blocks, dtype=jnp.int32)[:, None] * E_DEV + shuffled.astype(jnp.int32)).reshape(ELEMS)
    elem_of = jnp.zeros((ELEMS,), jnp.int32).at[slot_of].set(jnp.arange(ELEMS, dtype=jnp.int32))
    rotation = jax.random.randint(jax.random.fold_in(key, 8), (ELEMS,), 0, 4)
    flip_x = jax.random.randint(jax.random.fold_in(key, 9), (ELEMS,), 0, 2)
    flip_y = jax.random.randint(jax.random.fold_in(key, 10), (ELEMS,), 0, 2)
    column_pos = slot_of // EW
    row_pos = slot_of % EW
    direction = (jnp.arange(4, dtype=jnp.int32)[None, :] - rotation[:, None]) % 4
    west_slot = (column_pos - 1) % columns * EW + row_pos
    east_slot = (column_pos + 1) % columns * EW + row_pos
    south_slot = column_pos * EW + jnp.maximum(row_pos - 1, 0)
    north_slot = column_pos * EW + jnp.minimum(row_pos + 1, EW - 1)
    next_slot = jnp.where(direction == 0, west_slot[:, None], jnp.where(direction == 1, east_slot[:, None], jnp.where(direction == 2, south_slot[:, None], north_slot[:, None])))
    flip_bits = jnp.where(direction == 0, flip_x[west_slot][:, None], jnp.where(direction == 1, flip_x[slot_of][:, None], jnp.where(direction == 2, flip_y[south_slot][:, None], flip_y[slot_of][:, None])))
    at_wall = (direction == 2) & (row_pos[:, None] == 0) | (direction == 3) & (row_pos[:, None] == EW - 1)
    partner = elem_of[next_slot]
    far_side = (jnp.bitwise_xor(direction, 1) + rotation[partner]) % 4
    return (jnp.where(at_wall, -1, partner).astype(jnp.int32), jnp.where(at_wall, 0, far_side).astype(jnp.int32), jnp.where(at_wall, 0, flip_bits).astype(jnp.int32))


def draw_face_partner(key, part):
    return face_tables(key)[0]


def draw_face_side(key, part):
    return face_tables(key)[1]


def draw_face_flip(key, part):
    return face_tables(key)[2]


def draw_velocity_modes(key, part):
    dims_all = (3, PLANES, ELEMS, NPTS)
    raw = jnp.clip(jax.random.normal(key, dims_all, jnp.float32), -4.0, 4.0)
    wave_number = (jnp.arange(PLANES) // 2).astype(jnp.float32)
    degree_x = (jnp.arange(NPTS) // 12).astype(jnp.float32)
    degree_y = (jnp.arange(NPTS) % 12).astype(jnp.float32)
    decay = 0.2 / ((1.0 + wave_number / 16.0)[:, None, None] * ((1.0 + degree_x) * (1.0 + degree_y))[None, None, :])
    return (raw * decay[None]).astype(jnp.bfloat16)


def block_levels(stream_key, dims, shards, least, top_value):
    loudness, own = 1.0, jax.random.fold_in(stream_key, 6)
    for axis_at, shards_of in shards:
        steps = jnp.exp(jax.random.uniform(jax.random.fold_in(own, axis_at), (shards_of,), jnp.float32, least / len(shards), top_value / len(shards)))
        loudness = loudness * jnp.repeat(steps, dims[axis_at] // shards_of).reshape([-1 if axis == axis_at else 1 for axis in range(len(dims))])
    return loudness


def setup_inputs(seed: int = 0) -> dict:
    arg_keys = jax.random.split(jax.random.key(seed), 6)
    velocity_modes = draw_velocity_modes(jax.random.fold_in(arg_keys[5], 71), 0)
    metric = jnp.clip(jnp.exp(math.log(2.0) - 1.3862944 * jax.random.uniform(arg_keys[1], (ELEMS, 4), jnp.float32) ** block_levels(arg_keys[1], (ELEMS, 4), ((0, 64),), -0.2, 0.2)), 0.5, 2.0)
    face_partner = draw_face_partner(jax.random.fold_in(arg_keys[5], 71), 0)
    face_side = draw_face_side(jax.random.fold_in(arg_keys[5], 71), 0)
    face_flip = draw_face_flip(jax.random.fold_in(arg_keys[5], 71), 0)
    return dict(velocity_modes=velocity_modes, metric=metric, face_partner=face_partner, face_side=face_side, face_flip=face_flip)


def legendre_tables():
    node_points = -np.cos(np.pi * np.arange(12) / 11.0)
    values = np.zeros((12, 12))
    slopes = np.zeros((12, 12))
    values[:, 0] = 1.0
    values[:, 1] = node_points
    slopes[:, 1] = 1.0
    for degree in range(1, 11):
        values[:, degree + 1] = ((2 * degree + 1) * node_points * values[:, degree] - degree * values[:, degree - 1]) / (degree + 1)
        slopes[:, degree + 1] = slopes[:, degree - 1] + (2 * degree + 1) * values[:, degree]
    basis_table = np.kron(values, values).T
    along_xi = np.kron(slopes, values).T
    along_eta = np.kron(values, slopes).T
    return tuple(jnp.asarray(table, dtype=jnp.float32).astype(jnp.bfloat16) for table in (basis_table, along_xi, along_eta))


def fourier_tables(planes, phys):
    plane_index = jnp.arange(planes, dtype=jnp.int32)
    wave_number = plane_index // 2
    is_imag = (plane_index % 2) == 1
    point_index = jnp.arange(phys, dtype=jnp.int32)
    turn_count = (point_index[:, None] * wave_number[None, :]) % phys
    phase_angle = turn_count.astype(jnp.float32) * (2.0 * np.pi / phys)
    weight = jnp.where(wave_number == 0, 1.0, 2.0).astype(jnp.float32)
    inverse = jnp.where(is_imag[None, :], -weight[None, :] * jnp.sin(phase_angle), weight[None, :] * jnp.cos(phase_angle))
    forward = jnp.where(is_imag[None, :], -jnp.sin(phase_angle), jnp.cos(phase_angle)).T / phys
    return inverse.astype(jnp.bfloat16), forward.astype(jnp.bfloat16)


def element_fields(mode_block, geometry, tables):
    basis_table, along_xi, along_eta = tables
    point_values = jnp.dot(mode_block, basis_table, preferred_element_type=jnp.float32).astype(jnp.bfloat16)
    d_xi = jnp.dot(mode_block, along_xi, preferred_element_type=jnp.float32)
    d_eta = jnp.dot(mode_block, along_eta, preferred_element_type=jnp.float32)
    coef = [geometry[:, k][None, None, :, None] for k in range(4)]
    grad_x = d_xi * coef[0] + d_eta * coef[1]
    grad_y = d_xi * coef[2] + d_eta * coef[3]
    grads = jnp.stack([grad_x, grad_y], axis=1).astype(jnp.bfloat16)
    dims_in = mode_block.shape
    return point_values, grads.reshape(6, dims_in[1], dims_in[2], dims_in[3])


def face_traces(grads):
    fields, planes, elems, npts = grads.shape
    grid_view = grads.reshape(fields, planes, elems, 12, 12)
    face_rows = jnp.stack([grid_view[..., 0, :], grid_view[..., 11, :], grid_view[..., :, 0], grid_view[..., :, 11]], axis=3)
    return face_rows.transpose(2, 3, 4, 0, 1).reshape(elems, 4, 12, fields * planes)


def apply_average(grads, own_rows, other_rows, partner, flip):
    fields, planes, elems, npts = grads.shape
    other_rows = jnp.where(flip[:, :, None, None] == 1, other_rows[:, :, ::-1, :], other_rows)
    averaged = jnp.where(partner[:, :, None, None] >= 0, 0.5 * (own_rows.astype(jnp.float32) + other_rows.astype(jnp.float32)), own_rows.astype(jnp.float32)).astype(jnp.bfloat16)
    restored = averaged.reshape(elems, 4, 12, fields, planes).transpose(3, 4, 0, 1, 2)
    grid_view = grads.reshape(fields, planes, elems, 12, 12)
    grid_view = grid_view.at[..., 0, 1:11].set(restored[..., 0, 1:11])
    grid_view = grid_view.at[..., 11, 1:11].set(restored[..., 1, 1:11])
    grid_view = grid_view.at[..., 1:11, 0].set(restored[..., 2, 1:11])
    grid_view = grid_view.at[..., 1:11, 11].set(restored[..., 3, 1:11])
    return grid_view.reshape(fields, planes, elems, npts)


def z_gradients(values, first_plane):
    dims_in = values.shape
    paired = values.astype(jnp.float32).reshape(dims_in[0], dims_in[1] // 2, 2, -1)
    wave_number = (first_plane // 2 + jnp.arange(dims_in[1] // 2, dtype=jnp.int32)).astype(jnp.float32) / 32.0
    scale = wave_number[None, :, None]
    turned = jnp.stack([-scale * paired[:, :, 1], scale * paired[:, :, 0]], axis=2)
    return turned.reshape(dims_in).astype(jnp.bfloat16)


def advection(physical):
    terms = []
    for comp in range(3):
        term = physical[:, 0] * physical[:, 3 + 2 * comp] + physical[:, 1] * physical[:, 4 + 2 * comp] + physical[:, 2] * physical[:, 9 + comp]
        terms.append(term)
    return jnp.stack(terms, axis=1).astype(jnp.bfloat16)


def reference(velocity_modes, metric, face_partner, face_side, face_flip):
    tables = legendre_tables()
    inverse, forward = fourier_tables(PLANES, PHYS)
    blocks = ELEMS // E_DEV
    by_block = velocity_modes.reshape(3, PLANES, blocks, E_DEV, NPTS).transpose(2, 0, 1, 3, 4)
    metric_blocks = metric.reshape(blocks, E_DEV, 4)

    def traces_of(block_item):
        mode_block, geometry = block_item
        point_values, grads = element_fields(mode_block, geometry, tables)
        return face_traces(grads)

    all_traces = lax.map(traces_of, (by_block, metric_blocks)).reshape(ELEMS, 4, 12, 6 * PLANES)
    clipped = jnp.maximum(face_partner, 0).reshape(blocks, E_DEV, 4)

    def evaluate(block_item):
        mode_block, geometry, partner, far_side, flip, clip_block = block_item
        point_values, grads = element_fields(mode_block, geometry, tables)
        own_rows = face_traces(grads)
        other_rows = all_traces[clip_block, far_side]
        grads = apply_average(grads, own_rows, other_rows, partner, flip)
        z_grads = z_gradients(point_values, 0)
        fields = jnp.concatenate([point_values, grads, z_grads], axis=0).reshape(12, PLANES, E_DEV * NPTS)
        flattened = fields.transpose(1, 0, 2).reshape(PLANES, 12 * E_DEV * NPTS)
        physical = jnp.dot(inverse, flattened, preferred_element_type=jnp.float32).reshape(PHYS, 12, E_DEV * NPTS)
        adv = advection(physical)
        result = jnp.dot(forward, adv.reshape(PHYS, 3 * E_DEV * NPTS), preferred_element_type=jnp.float32).astype(jnp.bfloat16)
        return result.reshape(PLANES, 3, E_DEV, NPTS)

    outputs = lax.map(evaluate, (by_block, metric_blocks, face_partner.reshape(blocks, E_DEV, 4), face_side.reshape(blocks, E_DEV, 4), face_flip.reshape(blocks, E_DEV, 4), clipped))
    return outputs.transpose(2, 1, 0, 3, 4).reshape(3, PLANES, ELEMS, NPTS)
```

```python
import functools

import jax
import jax.numpy as jnp
import numpy as np
from jax import lax
from jax.experimental import pallas as pl
from jax.experimental.pallas import tpu as pltpu
from jax.sharding import PartitionSpec as P

F32, BF16 = jnp.float32, jnp.bfloat16
NT = (((1,), (1,)), ((), ()))
INTERPRET = False


def bf16(table):
    return jnp.asarray(np.asarray(table, np.float32)).astype(BF16)


def legendre_tables():
    points = -np.cos(np.pi * np.arange(12) / 11.0)
    values, slopes = np.zeros((12, 12)), np.zeros((12, 12))
    values[:, 0] = 1.0
    values[:, 1] = points
    slopes[:, 1] = 1.0
    for n in range(1, 11):
        values[:, n + 1] = ((2 * n + 1) * points * values[:, n] - n * values[:, n - 1]) / (n + 1)
        slopes[:, n + 1] = slopes[:, n - 1] + (2 * n + 1) * values[:, n]
    return np.kron(values, values), np.kron(slopes, values), np.kron(values, slopes)


def face_points(face):
    t = np.arange(12)
    return (t, 132 + t, 12 * t, 12 * t + 11)[face]


def trace_table():
    _, xi, eta = legendre_tables()
    table = np.zeros((272, 144))
    table[np.arange(16), 128 + np.arange(16)] = 1.0
    for face in range(4):
        q = face_points(face)
        for at, rows in ((16, xi[q]), (80, eta[q]), (144, xi[q[::-1]]), (208, eta[q[::-1]])):
            table[at + 16 * face : at + 16 * face + 12] = rows
    return table


def point_table():
    basis, xi, eta = legendre_tables()
    return np.stack([np.concatenate([t[72 * h : 72 * h + 72] for t in (basis, xi, eta)]) for h in range(2)])


def half_face_rows(h):
    own = [(h, t) for t in range(1, 11)]
    along = range(1, 6) if h == 0 else range(6, 11)
    return own + [(f, t) for f in (2, 3) for t in along]


def pick_table():
    table = np.zeros((80, 128))
    for h in range(2):
        for g in range(2):
            for i, (f, t) in enumerate(half_face_rows(h)):
                table[40 * h + 20 * g + i, 64 * g + 16 * f + t] = 1.0
    return table


def place_table():
    table = np.zeros((2, 144, 40))
    for h in range(2):
        for g in range(2):
            for i, (f, t) in enumerate(half_face_rows(h)):
                table[h, 72 * g + face_points(f)[t] - 72 * h, 20 * g + i] = 1.0
    return table


def fourier_tables(planes, phys):
    m = np.arange(planes) // 2
    odd = np.arange(planes) % 2 == 1
    theta = (2.0 * np.pi / phys) * ((np.arange(phys)[None, :] * m[:, None]) % phys)
    weight = np.where(m == 0, 1.0, 2.0)[:, None]
    synth = np.where(odd[:, None], -weight * np.sin(theta), weight * np.cos(theta))
    analysis = np.where(odd[:, None], -np.sin(theta), np.cos(theta)) / phys
    return synth, analysis


def iota(shape, axis):
    return lax.broadcasted_iota(jnp.int32, shape, axis)


def to_element_rows():
    out, inp = iota((128, 128), 0), iota((128, 128), 1)
    return jnp.where(inp == (out % 16) * 8 + out // 16, 1.0, 0.0).astype(BF16)


def reverse_faces():
    out, inp = iota((128, 128), 0), iota((128, 128), 1)
    t = out % 16
    return jnp.where((t < 12) & (inp == out - t + 11 - t), 1.0, 0.0).astype(BF16)


def dot(a, b):
    return jnp.dot(a, b, preferred_element_type=F32)


def dot_nt(a, b):
    return lax.dot_general(a, b, NT, preferred_element_type=F32)


def dot_tn(a, b):
    return lax.dot_general(a, b, (((0,), (0,)), ((), ())), preferred_element_type=F32)


def prev_next(where_ref, blocks):
    me = where_ref[0]
    return me, jnp.where(me == 0, blocks - 1, me - 1), jnp.where(me == blocks - 1, 0, me + 1)


def pack_kernel(blocks, where_ref, partner_ref, metric_ref, v_ref, table_ref, modal_ref, own_ref, prev_ref, next_ref, rows_ref):
    order = to_element_rows()
    rows_ref[:, 96:128, :] = jnp.zeros((8, 32, 144), BF16)
    for b in range(6):
        block = dot(order, v_ref[128 * b : 128 * b + 128, :]).astype(BF16)
        for e in range(8):
            rows_ref[e, 16 * b : 16 * b + 16, :] = block[16 * e : 16 * e + 16]
    table = table_ref[...]
    for e in range(8):
        rows = rows_ref[e]
        out = dot_nt(table, rows)
        tail = out[0:16].astype(BF16)
        for z in range(2):
            modal_ref[z, e, 0:96, :] = rows[0:96, 0:128]
            modal_ref[z, e, 96:112, :] = tail
        for flip in range(2):
            xi = out[16 + 128 * flip : 80 + 128 * flip]
            eta = out[80 + 128 * flip : 144 + 128 * flip]
            for g in range(2):
                grad = xi * metric_ref[e, 2 * g] + eta * metric_ref[e, 2 * g + 1]
                own_ref[e, flip, 64 * g : 64 * g + 64, :] = grad.astype(BF16)
    me, before, after = prev_next(where_ref, blocks)
    for side, out_ref in ((before, prev_ref), (after, next_ref)):
        low, high = jnp.int32(7), jnp.int32(0)
        for e in range(8):
            for f in range(4):
                p = partner_ref[e, f]
                there = (p >= 0) & (lax.shift_right_arithmetic(p, 3) == side)
                low = jnp.where(there, jnp.minimum(low, e), low)
                high = jnp.where(there, jnp.maximum(high, e), high)
        out_ref[0] = own_ref[low, 0]
        out_ref[1] = own_ref[high, 0]


def average_kernel(blocks, where_ref, partner_ref, side_ref, flip_ref, own_ref, prev_ref, next_ref, pick_ref, modal_ref, send_ref, all_ref):
    me, before, after = prev_next(where_ref, blocks)
    reverse = reverse_faces()
    all_ref[0:128] = own_ref[...].reshape(128, 16, 128)
    for k, ref in ((8, prev_ref), (10, next_ref)):
        for i in range(2):
            at = 16 * (k + i)
            all_ref[at : at + 8] = ref[i].reshape(8, 16, 128)
            all_ref[at + 8 : at + 16] = dot(reverse, ref[i]).astype(BF16).reshape(8, 16, 128)
    least = []
    for side in (before, after):
        low = jnp.int32(1 << 30)
        for e in range(8):
            for f in range(4):
                p = partner_ref[e, f]
                there = (p >= 0) & (lax.shift_right_arithmetic(p, 3) == side)
                low = jnp.where(there, jnp.minimum(low, p), low)
        least.append(low)
    pick = pick_ref[...]
    for e in range(8):
        tiles = [None] * 8
        for f in range(4):
            p = partner_ref[e, f]
            home = lax.shift_right_arithmetic(p, 3)
            slot = jnp.where(
                home == me,
                lax.bitwise_and(p, 7),
                jnp.where(home == before, 8 + (p != least[0]).astype(jnp.int32), 10 + (p != least[1]).astype(jnp.int32)),
            )
            place = jnp.where(p >= 0, slot * 16 + flip_ref[e, f] * 8 + side_ref[e, f], 16 * e + f)
            for g in range(2):
                own = all_ref[16 * e + 4 * g + f].astype(F32)
                other = all_ref[place + 4 * g].astype(F32)
                tiles[4 * g + f] = (0.5 * (own + other)).astype(BF16)
        out = dot(pick, jnp.concatenate(tiles, axis=0))
        for h in range(2):
            send_ref[h, e, 112:152, :] = out[40 * h : 40 * h + 40].astype(BF16)


def regroup(blocks):
    rows = blocks[0].shape[0]
    lane = iota((rows, 128), 1) // 32
    out = []
    for c in range(3):
        groups = []
        for first in range(0, len(blocks), 4):
            group = None
            for k in range(4):
                shift = (32 * (k - c)) % 128
                piece = pltpu.roll(blocks[first + k], shift, 1) if shift else blocks[first + k]
                group = piece if group is None else jnp.where(lane == k, piece, group)
            groups.append(group)
        out.append(jnp.concatenate(groups, axis=1))
    return out


def main_kernel(where_ref, metric_ref, got_ref, table_ref, place_ref, synth_ref, analysis_ref, out_ref, field_ref, adv_ref):
    elem, half = where_ref[1], where_ref[2]
    m = [metric_ref[elem, k] for k in range(4)]
    table = table_ref[half]
    place = place_ref[half]
    tails = regroup([got_ref[p, 96:112, :].astype(F32) for p in range(16)])
    faces = regroup([got_ref[p, 112:152, :].astype(F32) for p in range(16)])
    on_face = dot(place, jnp.ones((40, 512), BF16)) > 0.5
    lane = iota((72, 128), 1)
    even = lane % 2 == 0
    for c in range(3):
        modes = jnp.concatenate([got_ref[p, 32 * c : 32 * c + 32, :] for p in range(16)], axis=0)
        d = dot_nt(table[:, 0:128], modes) + dot(table[:, 128:144], tails[c].astype(BF16))
        value = d[0:72].astype(BF16).astype(F32)
        xi, eta = d[72:144], d[144:216]
        turned = []
        for g in range(4):
            v = value[:, 128 * g : 128 * g + 128]
            k = ((lane + 128 * g) // 2).astype(F32) * (1.0 / 32.0)
            turned.append(jnp.where(even, -k * pltpu.roll(v, 127, 1), k * pltpu.roll(v, 1, 1)))
        field_ref[288 * c : 288 * c + 144, :] = jnp.concatenate([value, jnp.concatenate(turned, axis=1)], axis=0).astype(BF16)
        grads = jnp.concatenate([xi * m[0] + eta * m[1], xi * m[2] + eta * m[3]], axis=0)
        grads = jnp.where(on_face, dot(place, faces[c].astype(BF16)), grads)
        field_ref[288 * c + 144 : 288 * c + 288, :] = grads.astype(BF16)
    adv_ref[208:256, :] = jnp.zeros((48, 768), BF16)
    for j in range(0, 768, 256):
        phys = dot(field_ref[...], synth_ref[:, j : j + 256])
        terms = []
        for c in range(3):
            at = 288 * c
            terms.append(
                phys[0:72] * phys[at + 144 : at + 216]
                + phys[288:360] * phys[at + 216 : at + 288]
                + phys[576:648] * phys[at + 72 : at + 144]
            )
        terms.append(jnp.zeros((8, 256), F32))
        adv_ref[0:224, j : j + 256] = jnp.concatenate(terms, axis=0).astype(BF16)
    out = dot_nt(analysis_ref[...], adv_ref[...])
    out_ref[...] = out.astype(BF16).reshape(16, 32, 256)


def unpack_kernel(in_ref, out_ref):
    order = to_element_rows()
    rows, cols = iota((256, 144), 0), iota((256, 144), 1)
    for c in range(3):
        block = None
        for z in range(2):
            pick = jnp.where((rows - 72 * c == cols - 72 * z) & (cols // 72 == z), 1.0, 0.0).astype(BF16)
            part = dot(in_ref[8 * z : 8 * z + 8].reshape(256, 256), pick)
            block = part if block is None else block + part
        block = block.astype(BF16)
        for b in range(2):
            piece = jnp.concatenate([block[32 * e + 16 * b : 32 * e + 16 * b + 16] for e in range(8)], axis=0)
            back = dot_tn(order, piece)
            at = 256 * c + 128 * b
            out_ref[at : at + 128, :] = back.astype(BF16)


SMEM = pl.BlockSpec(memory_space=pltpu.SMEM)
VMEM = pl.BlockSpec(memory_space=pltpu.VMEM)


def call(kernel, in_specs, out_shapes, scratch=(), aliases=None):
    single = not isinstance(out_shapes, (list, tuple)) or hasattr(out_shapes, "shape")
    return pl.pallas_call(
        kernel,
        in_specs=in_specs,
        out_specs=VMEM if single else [VMEM] * len(out_shapes),
        out_shape=out_shapes,
        scratch_shapes=list(scratch),
        compiler_params=pltpu.CompilerParams(vmem_limit_bytes=40 * 1024 * 1024),
        input_output_aliases=aliases or {},
        interpret=INTERPRET,
    )


def shape(*dims):
    return jax.ShapeDtypeStruct(dims, BF16)


def on_device(velocity_modes, metric, face_partner, face_side, face_flip):
    blocks = lax.axis_size("elem")
    position = lax.axis_index("plane")
    where = jnp.stack([lax.axis_index("elem"), position % 8, position // 8]).astype(jnp.int32)
    up = [(i, (i + 1) % blocks) for i in range(blocks)]
    down = [(j, i) for i, j in up]
    synth, analysis = fourier_tables(512, 768)
    modal, own, to_prev, to_next = call(
        functools.partial(pack_kernel, blocks),
        [SMEM, SMEM, SMEM, VMEM, VMEM],
        [shape(2, 8, 152, 128), shape(8, 2, 128, 128), shape(2, 128, 128), shape(2, 128, 128)],
        [pltpu.VMEM((8, 128, 144), BF16)],
    )(where, face_partner, metric, velocity_modes.reshape(768, 144), bf16(trace_table()))
    from_prev = lax.ppermute(to_next, "elem", up)
    from_next = lax.ppermute(to_prev, "elem", down)
    sent = call(
        functools.partial(average_kernel, blocks),
        [SMEM, SMEM, SMEM, SMEM, VMEM, VMEM, VMEM, VMEM, VMEM],
        shape(2, 8, 152, 128),
        [pltpu.VMEM((192, 16, 128), BF16)],
        {8: 0},
    )(where, face_partner, face_side, face_flip, own, from_prev, from_next, bf16(pick_table()), modal)
    got = lax.all_to_all(sent.reshape(16, 152, 128), "plane", 0, 0, tiled=True)
    out = call(
        main_kernel,
        [SMEM, SMEM, VMEM, VMEM, VMEM, VMEM, VMEM],
        shape(16, 32, 256),
        [pltpu.VMEM((864, 512), BF16), pltpu.VMEM((256, 768), BF16)],
    )(where, metric, got, bf16(point_table()), bf16(place_table()), bf16(synth), bf16(analysis))
    out = lax.all_to_all(out, "plane", 0, 0, tiled=True)
    out = call(unpack_kernel, [VMEM], shape(768, 144))(out)
    return out.reshape(3, 32, 8, 144)


def solution(mesh):
    by_elem = P("elem", None)
    whole = P(None, "plane", "elem", None)
    return jax.shard_map(
        on_device,
        mesh=mesh,
        in_specs=(whole, by_elem, by_elem, by_elem, by_elem),
        out_specs=whole,
        check_vma=False,
    )
```

```python
import functools

import jax
import jax.numpy as jnp
import numpy as np
from jax import lax
from jax.experimental import pallas as pl
from jax.experimental.pallas import tpu as pltpu
from jax.sharding import PartitionSpec as P


F32, BF16 = jnp.float32, jnp.bfloat16
NT = (((1,), (1,)), ((), ()))
INTERPRET = False


def bf16(table):
    return jnp.asarray(np.asarray(table, np.float32)).astype(BF16)


def legendre_tables():
    points = -np.cos(np.pi * np.arange(12) / 11.0)
    values, slopes = np.zeros((12, 12)), np.zeros((12, 12))
    values[:, 0] = 1.0
    values[:, 1] = points
    slopes[:, 1] = 1.0
    for n in range(1, 11):
        values[:, n + 1] = ((2 * n + 1) * points * values[:, n] - n * values[:, n - 1]) / (n + 1)
        slopes[:, n + 1] = slopes[:, n - 1] + (2 * n + 1) * values[:, n]
    return np.kron(values, values), np.kron(slopes, values), np.kron(values, slopes)


def face_points(face):
    t = np.arange(12)
    return (t, 132 + t, 12 * t, 12 * t + 11)[face]


def trace_table():
    _, xi, eta = legendre_tables()
    table = np.zeros((272, 144))
    table[np.arange(16), 128 + np.arange(16)] = 1.0
    for face in range(4):
        q = face_points(face)
        for at, rows in ((16, xi[q]), (80, eta[q]), (144, xi[q[::-1]]), (208, eta[q[::-1]])):
            table[at + 16 * face : at + 16 * face + 12] = rows
    return table


def point_table():
    basis, xi, eta = legendre_tables()
    return np.stack([np.concatenate([t[72 * h : 72 * h + 72] for t in (basis, xi, eta)]) for h in range(2)])


def half_face_rows(h):
    own = [(h, t) for t in range(1, 11)]
    along = range(1, 6) if h == 0 else range(6, 11)
    return own + [(f, t) for f in (2, 3) for t in along]


def pick_table():
    table = np.zeros((80, 128))
    for h in range(2):
        for g in range(2):
            for i, (f, t) in enumerate(half_face_rows(h)):
                table[40 * h + 20 * g + i, 64 * g + 16 * f + t] = 1.0
    return table


def place_table():
    table = np.zeros((2, 144, 40))
    for h in range(2):
        for g in range(2):
            for i, (f, t) in enumerate(half_face_rows(h)):
                table[h, 72 * g + face_points(f)[t] - 72 * h, 20 * g + i] = 1.0
    return table


def fourier_tables(planes, phys):
    m = np.arange(planes) // 2
    odd = np.arange(planes) % 2 == 1
    theta = (2.0 * np.pi / phys) * ((np.arange(phys)[None, :] * m[:, None]) % phys)
    weight = np.where(m == 0, 1.0, 2.0)[:, None]
    synth = np.where(odd[:, None], -weight * np.sin(theta), weight * np.cos(theta))
    analysis = np.where(odd[:, None], -np.sin(theta), np.cos(theta)) / phys
    return synth, analysis


def iota(shape, axis):
    return lax.broadcasted_iota(jnp.int32, shape, axis)


def to_element_rows():
    out, inp = iota((128, 128), 0), iota((128, 128), 1)
    return jnp.where(inp == (out % 16) * 8 + out // 16, 1.0, 0.0).astype(BF16)


def reverse_faces():
    out, inp = iota((128, 128), 0), iota((128, 128), 1)
    t = out % 16
    return jnp.where((t < 12) & (inp == out - t + 11 - t), 1.0, 0.0).astype(BF16)


def dot(a, b):
    return jnp.dot(a, b, preferred_element_type=F32)


def dot_nt(a, b):
    return lax.dot_general(a, b, NT, preferred_element_type=F32)


def dot_tn(a, b):
    return lax.dot_general(a, b, (((0,), (0,)), ((), ())), preferred_element_type=F32)


def prev_next(where_ref, blocks):
    me = where_ref[0]
    return me, jnp.where(me == 0, blocks - 1, me - 1), jnp.where(me == blocks - 1, 0, me + 1)


def pack_kernel(blocks, where_ref, partner_ref, metric_ref, v_ref, table_ref, modal_ref, own_ref, prev_ref, next_ref, rows_ref):
    order = to_element_rows()
    rows_ref[:, 96:128, :] = jnp.zeros((8, 32, 144), BF16)
    for b in range(6):
        block = dot(order, v_ref[128 * b : 128 * b + 128, :]).astype(BF16)
        for e in range(8):
            rows_ref[e, 16 * b : 16 * b + 16, :] = block[16 * e : 16 * e + 16]
    table = table_ref[...]
    for e in range(8):
        rows = rows_ref[e]
        out = dot_nt(table, rows)
        tail = out[0:16].astype(BF16)
        for z in range(2):
            modal_ref[z, e, 0:96, :] = rows[0:96, 0:128]
            modal_ref[z, e, 96:112, :] = tail
        for flip in range(2):
            xi = out[16 + 128 * flip : 80 + 128 * flip]
            eta = out[80 + 128 * flip : 144 + 128 * flip]
            for g in range(2):
                grad = xi * metric_ref[e, 2 * g] + eta * metric_ref[e, 2 * g + 1]
                own_ref[e, flip, 64 * g : 64 * g + 64, :] = grad.astype(BF16)
    _, before, after = prev_next(where_ref, blocks)
    for side, out_ref in ((before, prev_ref), (after, next_ref)):
        low, high = jnp.int32(7), jnp.int32(0)
        for e in range(8):
            for f in range(4):
                p = partner_ref[e, f]
                there = (p >= 0) & (lax.shift_right_arithmetic(p, 3) == side)
                low = jnp.where(there, jnp.minimum(low, e), low)
                high = jnp.where(there, jnp.maximum(high, e), high)
        out_ref[0] = own_ref[low, 0]
        out_ref[1] = own_ref[high, 0]


def average_kernel(blocks, where_ref, partner_ref, side_ref, flip_ref, own_ref, prev_ref, next_ref, pick_ref, face_ref, all_ref):
    me, before, after = prev_next(where_ref, blocks)
    reverse = reverse_faces()
    all_ref[0:128] = own_ref[...].reshape(128, 16, 128)
    for k, ref in ((8, prev_ref), (10, next_ref)):
        for i in range(2):
            at = 16 * (k + i)
            all_ref[at : at + 8] = ref[i].reshape(8, 16, 128)
            all_ref[at + 8 : at + 16] = dot(reverse, ref[i]).astype(BF16).reshape(8, 16, 128)
    least = []
    for side in (before, after):
        low = jnp.int32(1 << 30)
        for e in range(8):
            for f in range(4):
                p = partner_ref[e, f]
                there = (p >= 0) & (lax.shift_right_arithmetic(p, 3) == side)
                low = jnp.where(there, jnp.minimum(low, p), low)
        least.append(low)
    pick = pick_ref[...]
    for e in range(8):
        tiles = [None] * 8
        for f in range(4):
            p = partner_ref[e, f]
            home = lax.shift_right_arithmetic(p, 3)
            slot = jnp.where(
                home == me,
                lax.bitwise_and(p, 7),
                jnp.where(home == before, 8 + (p != least[0]).astype(jnp.int32), 10 + (p != least[1]).astype(jnp.int32)),
            )
            place = jnp.where(p >= 0, slot * 16 + flip_ref[e, f] * 8 + side_ref[e, f], 16 * e + f)
            for g in range(2):
                own = all_ref[16 * e + 4 * g + f].astype(F32)
                other = all_ref[place + 4 * g].astype(F32)
                tiles[4 * g + f] = (0.5 * (own + other)).astype(BF16)
        out = dot(pick, jnp.concatenate(tiles, axis=0))
        for h in range(2):
            face_ref[h, e] = out[40 * h : 40 * h + 40].astype(BF16)


def regroup(blocks):
    rows = blocks[0].shape[0]
    lane = iota((rows, 128), 1) // 32
    out = []
    for c in range(3):
        groups = []
        for first in range(0, len(blocks), 4):
            group = None
            for k in range(4):
                shift = (32 * (k - c)) % 128
                piece = pltpu.roll(blocks[first + k], shift, 1) if shift else blocks[first + k]
                group = piece if group is None else jnp.where(lane == k, piece, group)
            groups.append(group)
        out.append(jnp.concatenate(groups, axis=1))
    return out


def main_kernel(where_ref, metric_ref, modal_ref, face_ref, table_ref, place_ref, synth_ref, analysis_ref, out_ref, field_ref, adv_ref):
    elem, half = where_ref[1], where_ref[2]
    m = [metric_ref[elem, k] for k in range(4)]
    table = table_ref[half]
    place = place_ref[half]
    tails = regroup([modal_ref[p, 96:112, :].astype(F32) for p in range(16)])
    faces = regroup([face_ref[p].astype(F32) for p in range(16)])
    on_face = dot(place, jnp.ones((40, 512), BF16)) > 0.5
    lane = iota((72, 128), 1)
    even = lane % 2 == 0
    for c in range(3):
        modes = jnp.concatenate([modal_ref[p, 32 * c : 32 * c + 32, :] for p in range(16)], axis=0)
        d = dot_nt(table[:, 0:128], modes) + dot(table[:, 128:144], tails[c].astype(BF16))
        value = d[0:72].astype(BF16).astype(F32)
        xi, eta = d[72:144], d[144:216]
        turned = []
        for g in range(4):
            v = value[:, 128 * g : 128 * g + 128]
            k = ((lane + 128 * g) // 2).astype(F32) * (1.0 / 32.0)
            turned.append(jnp.where(even, -k * pltpu.roll(v, 127, 1), k * pltpu.roll(v, 1, 1)))
        field_ref[288 * c : 288 * c + 144, :] = jnp.concatenate([value, jnp.concatenate(turned, axis=1)], axis=0).astype(BF16)
        grads = jnp.concatenate([xi * m[0] + eta * m[1], xi * m[2] + eta * m[3]], axis=0)
        grads = jnp.where(on_face, dot(place, faces[c].astype(BF16)), grads)
        field_ref[288 * c + 144 : 288 * c + 288, :] = grads.astype(BF16)
    adv_ref[208:256, :] = jnp.zeros((48, 768), BF16)
    for j in range(0, 768, 256):
        phys = dot(field_ref[...], synth_ref[:, j : j + 256])
        terms = []
        for c in range(3):
            at = 288 * c
            terms.append(
                phys[0:72] * phys[at + 144 : at + 216]
                + phys[288:360] * phys[at + 216 : at + 288]
                + phys[576:648] * phys[at + 72 : at + 144]
            )
        terms.append(jnp.zeros((8, 256), F32))
        adv_ref[0:224, j : j + 256] = jnp.concatenate(terms, axis=0).astype(BF16)
    out = dot_nt(analysis_ref[...], adv_ref[...])
    out_ref[...] = out.astype(BF16).reshape(16, 32, 256)


def unpack_kernel(in_ref, out_ref):
    order = to_element_rows()
    rows, cols = iota((256, 144), 0), iota((256, 144), 1)
    for c in range(3):
        block = None
        for z in range(2):
            pick = jnp.where((rows - 72 * c == cols - 72 * z) & (cols // 72 == z), 1.0, 0.0).astype(BF16)
            part = dot(in_ref[8 * z : 8 * z + 8].reshape(256, 256), pick)
            block = part if block is None else block + part
        block = block.astype(BF16)
        for b in range(2):
            piece = jnp.concatenate([block[32 * e + 16 * b : 32 * e + 16 * b + 16] for e in range(8)], axis=0)
            back = dot_tn(order, piece)
            at = 256 * c + 128 * b
            out_ref[at : at + 128, :] = back.astype(BF16)


SMEM = pl.BlockSpec(memory_space=pltpu.SMEM)
VMEM = pl.BlockSpec(memory_space=pltpu.VMEM)


def call(kernel, in_specs, out_shapes, scratch=()):
    single = not isinstance(out_shapes, (list, tuple)) or hasattr(out_shapes, "shape")
    return pl.pallas_call(
        kernel,
        in_specs=in_specs,
        out_specs=VMEM if single else [VMEM] * len(out_shapes),
        out_shape=out_shapes,
        scratch_shapes=list(scratch),
        compiler_params=pltpu.CompilerParams(vmem_limit_bytes=40 * 1024 * 1024),
        interpret=INTERPRET,
    )


def shape(*dims):
    return jax.ShapeDtypeStruct(dims, BF16)


def on_device(velocity_modes, metric, face_partner, face_side, face_flip):
    blocks = lax.axis_size("elem")
    position = lax.axis_index("plane")
    where = jnp.stack([lax.axis_index("elem"), position % 8, position // 8]).astype(jnp.int32)
    up = [(i, (i + 1) % blocks) for i in range(blocks)]
    down = [(j, i) for i, j in up]
    synth, analysis = fourier_tables(512, 768)
    modal, own, to_prev, to_next = call(
        functools.partial(pack_kernel, blocks),
        [SMEM, SMEM, SMEM, VMEM, VMEM],
        [shape(2, 8, 112, 128), shape(8, 2, 128, 128), shape(2, 128, 128), shape(2, 128, 128)],
        [pltpu.VMEM((8, 128, 144), BF16)],
    )(where, face_partner, metric, velocity_modes.reshape(768, 144), bf16(trace_table()))
    from_prev = lax.ppermute(to_next, "elem", up)
    from_next = lax.ppermute(to_prev, "elem", down)
    modal = lax.all_to_all(modal.reshape(16, 112, 128), "plane", 0, 0, tiled=True)
    faces = call(
        functools.partial(average_kernel, blocks),
        [SMEM, SMEM, SMEM, SMEM, VMEM, VMEM, VMEM, VMEM],
        shape(2, 8, 40, 128),
        [pltpu.VMEM((192, 16, 128), BF16)],
    )(where, face_partner, face_side, face_flip, own, from_prev, from_next, bf16(pick_table()))
    faces = lax.all_to_all(faces.reshape(16, 40, 128), "plane", 0, 0, tiled=True)
    out = call(
        main_kernel,
        [SMEM, SMEM, VMEM, VMEM, VMEM, VMEM, VMEM, VMEM],
        shape(16, 32, 256),
        [pltpu.VMEM((864, 512), BF16), pltpu.VMEM((256, 768), BF16)],
    )(where, metric, modal, faces, bf16(point_table()), bf16(place_table()), bf16(synth), bf16(analysis))
    out = lax.all_to_all(out, "plane", 0, 0, tiled=True)
    out = call(unpack_kernel, [VMEM], shape(768, 144))(out)
    return out.reshape(3, 32, 8, 144)


def solution(mesh):
    by_elem = P("elem", None)
    whole = P(None, "plane", "elem", None)
    return jax.shard_map(
        on_device,
        mesh=mesh,
        in_specs=(whole, by_elem, by_elem, by_elem, by_elem),
        out_specs=whole,
        check_vma=False,
    )
```

```python
import functools

import jax
import jax.numpy as jnp
import numpy as np
from jax import lax
from jax.experimental import pallas as pl
from jax.experimental.pallas import tpu as pltpu
from jax.sharding import PartitionSpec as P

F32, BF16 = jnp.float32, jnp.bfloat16
NT = (((1,), (1,)), ((), ()))
INTERPRET = False


def bf16(table):
    return jnp.asarray(np.asarray(table, np.float32)).astype(BF16)


def legendre_tables():
    points = -np.cos(np.pi * np.arange(12) / 11.0)
    values, slopes = np.zeros((12, 12)), np.zeros((12, 12))
    values[:, 0] = 1.0
    values[:, 1] = points
    slopes[:, 1] = 1.0
    for n in range(1, 11):
        values[:, n + 1] = ((2 * n + 1) * points * values[:, n] - n * values[:, n - 1]) / (n + 1)
        slopes[:, n + 1] = slopes[:, n - 1] + (2 * n + 1) * values[:, n]
    return np.kron(values, values), np.kron(slopes, values), np.kron(values, slopes)


def face_points(face):
    t = np.arange(12)
    return (t, 132 + t, 12 * t, 12 * t + 11)[face]


def trace_table():
    _, xi, eta = legendre_tables()
    table = np.zeros((272, 144))
    table[np.arange(16), 128 + np.arange(16)] = 1.0
    for face in range(4):
        q = face_points(face)
        for at, rows in ((16, xi[q]), (80, eta[q]), (144, xi[q[::-1]]), (208, eta[q[::-1]])):
            table[at + 16 * face : at + 16 * face + 12] = rows
    return table


def point_table():
    basis, xi, eta = legendre_tables()
    return np.stack([np.concatenate([t[72 * h : 72 * h + 72] for t in (basis, xi, eta)]) for h in range(2)])


def half_face_rows(h):
    own = [(h, t) for t in range(1, 11)]
    along = range(1, 6) if h == 0 else range(6, 11)
    return own + [(f, t) for f in (2, 3) for t in along]


def pick_table():
    table = np.zeros((80, 128))
    for h in range(2):
        for g in range(2):
            for i, (f, t) in enumerate(half_face_rows(h)):
                table[40 * h + 20 * g + i, 64 * g + 16 * f + t] = 1.0
    return table


def place_table():
    table = np.zeros((2, 144, 40))
    for h in range(2):
        for g in range(2):
            for i, (f, t) in enumerate(half_face_rows(h)):
                table[h, 72 * g + face_points(f)[t] - 72 * h, 20 * g + i] = 1.0
    return table


def fourier_tables(planes, phys):
    m = np.arange(planes) // 2
    odd = np.arange(planes) % 2 == 1
    theta = (2.0 * np.pi / phys) * ((np.arange(phys)[None, :] * m[:, None]) % phys)
    weight = np.where(m == 0, 1.0, 2.0)[:, None]
    synth = np.where(odd[:, None], -weight * np.sin(theta), weight * np.cos(theta))
    analysis = np.where(odd[:, None], -np.sin(theta), np.cos(theta)) / phys
    return synth, analysis


def iota(shape, axis):
    return lax.broadcasted_iota(jnp.int32, shape, axis)


def to_element_rows():
    out, inp = iota((128, 128), 0), iota((128, 128), 1)
    return jnp.where(inp == ((out & 15) << 3) + (out >> 4), 1.0, 0.0).astype(BF16)


def reverse_faces():
    out, inp = iota((128, 128), 0), iota((128, 128), 1)
    t = out & 15
    return jnp.where((t < 12) & (inp == out - t + 11 - t), 1.0, 0.0).astype(BF16)


def dot(a, b):
    return jnp.dot(a, b, preferred_element_type=F32)


def dot_nt(a, b):
    return lax.dot_general(a, b, NT, preferred_element_type=F32)


def dot_tn(a, b):
    return lax.dot_general(a, b, (((0,), (0,)), ((), ())), preferred_element_type=F32)


def prev_next(where_ref, blocks):
    me = where_ref[0]
    return me, jnp.where(me == 0, blocks - 1, me - 1), jnp.where(me == blocks - 1, 0, me + 1)


def trace_kernel(blocks, where_ref, partner_hbm, metric_hbm, v_hbm, table_hbm, rows_ref, tail_ref, own_ref, prev_ref, next_ref, partner_ref, metric_ref, v_ref, table_ref, sems):
    copies = [
        pltpu.make_async_copy(src, dst, sems.at[i])
        for i, (src, dst) in enumerate(((v_hbm, v_ref), (table_hbm, table_ref), (metric_hbm, metric_ref), (partner_hbm, partner_ref)))
    ]
    for copy in copies:
        copy.start()
    order = to_element_rows()
    rows_ref[:, 96:128, :] = jnp.zeros((8, 32, 144), BF16)
    for copy in copies:
        copy.wait()
    for b in range(6):
        block = dot(order, v_ref[128 * b : 128 * b + 128, :]).astype(BF16)
        for e in range(8):
            rows_ref[e, 16 * b : 16 * b + 16, :] = block[16 * e : 16 * e + 16]
    table = table_ref[...]
    for e in range(8):
        out = dot_nt(table, rows_ref[e])
        tail_ref[e] = out[0:16].astype(BF16)
        for flip in range(2):
            xi = out[16 + 128 * flip : 80 + 128 * flip]
            eta = out[80 + 128 * flip : 144 + 128 * flip]
            for g in range(2):
                grad = xi * metric_ref[2 * g, e] + eta * metric_ref[2 * g + 1, e]
                at = 16 * e + 8 * flip + 4 * g
                own_ref[at : at + 4] = grad.astype(BF16).reshape(4, 16, 128)
    _, before, after = prev_next(where_ref, blocks)
    for side, out_ref in ((before, prev_ref), (after, next_ref)):
        low, high = jnp.int32(7), jnp.int32(0)
        for e in range(8):
            there = [(partner_ref[f, e] >= 0) & (lax.shift_right_arithmetic(partner_ref[f, e], 3) == side) for f in range(4)]
            there = (there[0] | there[1]) | (there[2] | there[3])
            low = jnp.where(there, jnp.minimum(low, e), low)
            high = jnp.where(there, jnp.maximum(high, e), high)
        out_ref[0] = own_ref[pl.ds(16 * low, 8)]
        out_ref[1] = own_ref[pl.ds(16 * high, 8)]


def average(own_ref, pick, element, places):
    tiles = [None] * 8
    for f in range(4):
        for g in range(2):
            own = own_ref[16 * element + 4 * g + f].astype(F32)
            other = own_ref[places[f] + 4 * g].astype(F32)
            tiles[4 * g + f] = (0.5 * (own + other)).astype(BF16)
    return dot(pick, jnp.concatenate(tiles, axis=0))


def pack_kernel(blocks, where_ref, partner_ref, side_ref, flip_ref, rows_ref, tail_ref, own_ref, pick_ref, send_ref, plan_ref, place_ref):
    me, before, after = prev_next(where_ref, blocks)
    sides = (before, after)
    low, high, least = [jnp.int32(7)] * 2, [jnp.int32(0)] * 2, [jnp.int32(1 << 30)] * 2
    for e in range(8):
        for f in range(4):
            p = partner_ref[f, e]
            for i in range(2):
                there = (p >= 0) & (lax.shift_right_arithmetic(p, 3) == sides[i])
                low[i] = jnp.where(there, jnp.minimum(low[i], e), low[i])
                high[i] = jnp.where(there, jnp.maximum(high[i], e), high[i])
                least[i] = jnp.where(there, jnp.minimum(least[i], p), least[i])
    pick = pick_ref[...]
    for e in range(8):
        places = []
        for f in range(4):
            p = partner_ref[f, e]
            home = lax.shift_right_arithmetic(p, 3)
            turn = flip_ref[f, e] * 8 + side_ref[f, e]
            near = lax.bitwise_and(p, 7) * 16 + turn
            far = jnp.where(home == before, jnp.where(p == least[0], 128, 144), jnp.where(p == least[1], 160, 176)) + turn
            place_ref[e, f] = jnp.where(p < 0, 16 * e + f, jnp.where(home == me, near, far))
            places.append(jnp.where(home == me, near, 16 * e + f))
        out = average(own_ref, pick, e, places)
        for h in range(2):
            send_ref[h, e, 0:96, :] = rows_ref[e, 0:96, 0:128]
            send_ref[h, e, 96:112, :] = tail_ref[e]
            send_ref[h, e, 112:152, :] = out[40 * h : 40 * h + 40].astype(BF16)
    for r, e in enumerate((low[0], high[0], low[1], high[1])):
        plan_ref[8 * r] = e
        for f in range(4):
            plan_ref[8 * r + 1 + f] = place_ref[e, f]


def border_kernel(plan_ref, prev_ref, next_ref, pick_ref, own_in, send_in, own_ref, send_ref):
    reverse = reverse_faces()
    for k, ref in ((8, prev_ref), (10, next_ref)):
        for i in range(2):
            at = 16 * (k + i)
            own_ref[at : at + 8] = ref[i]
            own_ref[at + 8 : at + 16] = dot(reverse, ref[i].reshape(128, 128)).astype(BF16).reshape(8, 16, 128)
    pick = pick_ref[...]
    for r in range(4):
        e = plan_ref[8 * r]
        out = average(own_ref, pick, e, [plan_ref[8 * r + 1 + f] for f in range(4)])
        for h in range(2):
            send_ref[h, e, 112:152, :] = out[40 * h : 40 * h + 40].astype(BF16)


def regroup(blocks):
    rows = blocks[0].shape[0]
    lane = iota((rows, 128), 1) >> 5
    out = []
    for c in range(3):
        groups = []
        for first in range(0, len(blocks), 4):
            group = None
            for k in range(4):
                shift = (32 * (k - c)) % 128
                piece = pltpu.roll(blocks[first + k], shift, 1) if shift else blocks[first + k]
                group = piece if group is None else jnp.where(lane == k, piece, group)
            groups.append(group)
        out.append(jnp.concatenate(groups, axis=1))
    return out


def main_kernel(where_ref, metric_ref, got_ref, table_ref, place_ref, synth_ref, analysis_ref, out_ref, field_ref, adv_ref):
    elem, half = where_ref[1], where_ref[2]
    m = [metric_ref[k, elem] for k in range(4)]
    table = table_ref[half]
    place = place_ref[half]
    tails = regroup([got_ref[p, 96:112, :].astype(F32) for p in range(16)])
    faces = regroup([got_ref[p, 112:152, :].astype(F32) for p in range(16)])
    on_face = dot(place, jnp.ones((40, 512), BF16)) > 0.5
    lane = iota((72, 128), 1)
    even = (lane & 1) == 0
    for c in range(3):
        modes = jnp.concatenate([got_ref[p, 32 * c : 32 * c + 32, :] for p in range(16)], axis=0)
        d = dot_nt(table[:, 0:128], modes) + dot(table[:, 128:144], tails[c].astype(BF16))
        value = d[0:72].astype(BF16).astype(F32)
        xi, eta = d[72:144], d[144:216]
        turned = []
        for g in range(4):
            v = value[:, 128 * g : 128 * g + 128]
            k = ((lane + 128 * g) >> 1).astype(F32) * (1.0 / 32.0)
            turned.append(jnp.where(even, -k * pltpu.roll(v, 127, 1), k * pltpu.roll(v, 1, 1)))
        field_ref[288 * c : 288 * c + 144, :] = jnp.concatenate([value, jnp.concatenate(turned, axis=1)], axis=0).astype(BF16)
        grads = jnp.concatenate([xi * m[0] + eta * m[1], xi * m[2] + eta * m[3]], axis=0)
        grads = jnp.where(on_face, dot(place, faces[c].astype(BF16)), grads)
        field_ref[288 * c + 144 : 288 * c + 288, :] = grads.astype(BF16)
    adv_ref[208:256, :] = jnp.zeros((48, 768), BF16)
    for j in range(0, 768, 256):
        phys = dot(field_ref[...], synth_ref[:, j : j + 256])
        terms = []
        for c in range(3):
            at = 288 * c
            terms.append(
                phys[0:72] * phys[at + 144 : at + 216]
                + phys[288:360] * phys[at + 216 : at + 288]
                + phys[576:648] * phys[at + 72 : at + 144]
            )
        terms.append(jnp.zeros((8, 256), F32))
        adv_ref[0:224, j : j + 256] = jnp.concatenate(terms, axis=0).astype(BF16)
    out = dot_nt(analysis_ref[...], adv_ref[...])
    out_ref[...] = out.astype(BF16).reshape(16, 32, 256)


def unpack_kernel(in_ref, out_ref):
    order = to_element_rows()
    lead, cols = iota((256, 144), 0) - iota((256, 144), 1), iota((256, 144), 1)
    mine = (cols < 72, cols >= 72)
    for c in range(3):
        block = None
        for z in range(2):
            pick = jnp.where((lead == 72 * (c - z)) & mine[z], 1.0, 0.0).astype(BF16)
            part = dot(in_ref[8 * z : 8 * z + 8].reshape(256, 256), pick)
            block = part if block is None else block + part
        block = block.astype(BF16)
        for b in range(2):
            piece = jnp.concatenate([block[32 * e + 16 * b : 32 * e + 16 * b + 16] for e in range(8)], axis=0)
            back = dot_tn(order, piece)
            at = 256 * c + 128 * b
            out_ref[at : at + 128, :] = back.astype(BF16)


SMEM = pl.BlockSpec(memory_space=pltpu.SMEM)
VMEM = pl.BlockSpec(memory_space=pltpu.VMEM)
HBM = pl.BlockSpec(memory_space=pltpu.HBM)


def call(kernel, in_specs, out_shapes, scratch=(), aliases=None, out_specs=None):
    single = not isinstance(out_shapes, (list, tuple)) or hasattr(out_shapes, "shape")
    return pl.pallas_call(
        kernel,
        in_specs=in_specs,
        out_specs=out_specs or (VMEM if single else [VMEM] * len(out_shapes)),
        out_shape=out_shapes,
        scratch_shapes=list(scratch),
        compiler_params=pltpu.CompilerParams(vmem_limit_bytes=40 * 1024 * 1024),
        input_output_aliases=aliases or {},
        interpret=INTERPRET,
    )


def in_hbm(x):
    return x if INTERPRET else pltpu.with_memory_space_constraint(x, pltpu.HBM)


def shape(*dims):
    return jax.ShapeDtypeStruct(dims, BF16)


def on_device(velocity_modes, metric, face_partner, face_side, face_flip):
    blocks = lax.axis_size("elem")
    position = lax.axis_index("plane")
    where = jnp.stack([lax.axis_index("elem"), position % 8, position // 8]).astype(jnp.int32)
    up = [(i, (i + 1) % blocks) for i in range(blocks)]
    down = [(j, i) for i, j in up]
    synth, analysis = fourier_tables(512, 768)
    partner, side, flip, geometry = face_partner.T, face_side.T, face_flip.T, metric.T
    pick = bf16(pick_table())
    rows, tail, own, to_prev, to_next = call(
        functools.partial(trace_kernel, blocks),
        [SMEM, HBM, HBM, HBM, HBM],
        [shape(8, 128, 144), shape(8, 16, 128), shape(192, 16, 128), shape(2, 8, 16, 128), shape(2, 8, 16, 128)],
        [pltpu.SMEM((4, 8), jnp.int32), pltpu.SMEM((4, 8), F32), pltpu.VMEM((768, 144), BF16), pltpu.VMEM((272, 144), BF16), pltpu.SemaphoreType.DMA((4,))],
    )(where, *map(in_hbm, (partner, geometry, velocity_modes.reshape(768, 144), bf16(trace_table()))))
    from_prev = lax.ppermute(to_next, "elem", up)
    from_next = lax.ppermute(to_prev, "elem", down)
    send, plan = call(
        functools.partial(pack_kernel, blocks),
        [SMEM, SMEM, SMEM, SMEM, VMEM, VMEM, VMEM, VMEM],
        [shape(2, 8, 152, 128), jax.ShapeDtypeStruct((32,), jnp.int32)],
        [pltpu.SMEM((8, 4), jnp.int32)],
        out_specs=[VMEM, SMEM],
    )(where, partner, side, flip, rows, tail, own, pick)
    _, send = call(
        border_kernel,
        [SMEM, VMEM, VMEM, VMEM, VMEM, VMEM],
        [shape(192, 16, 128), shape(2, 8, 152, 128)],
        aliases={4: 0, 5: 1},
    )(plan, from_prev, from_next, pick, own, send)
    got = lax.all_to_all(send.reshape(16, 152, 128), "plane", 0, 0, tiled=True)
    out = call(
        main_kernel,
        [SMEM, SMEM, VMEM, VMEM, VMEM, VMEM, VMEM],
        shape(16, 32, 256),
        [pltpu.VMEM((864, 512), BF16), pltpu.VMEM((256, 768), BF16)],
    )(where, geometry, got, bf16(point_table()), bf16(place_table()), bf16(synth), bf16(analysis))
    out = lax.all_to_all(out, "plane", 0, 0, tiled=True)
    out = call(unpack_kernel, [VMEM], shape(768, 144))(out)
    return out.reshape(3, 32, 8, 144)


def solution(mesh):
    by_elem = P("elem", None)
    whole = P(None, "plane", "elem", None)
    return jax.shard_map(
        on_device,
        mesh=mesh,
        in_specs=(whole, by_elem, by_elem, by_elem, by_elem),
        out_specs=whole,
        check_vma=False,
    )
```

```python
import functools

import jax
import jax.numpy as jnp
import numpy as np
from jax import lax
from jax.experimental import pallas as pl
from jax.experimental.pallas import tpu as pltpu
from jax.sharding import PartitionSpec as P

F32, BF16 = jnp.float32, jnp.bfloat16
NT = (((1,), (1,)), ((), ()))
INTERPRET = False


def bf16(table):
    return jnp.asarray(np.asarray(table, np.float32)).astype(BF16)


def legendre_tables():
    points = -np.cos(np.pi * np.arange(12) / 11.0)
    values, slopes = np.zeros((12, 12)), np.zeros((12, 12))
    values[:, 0] = 1.0
    values[:, 1] = points
    slopes[:, 1] = 1.0
    for n in range(1, 11):
        values[:, n + 1] = ((2 * n + 1) * points * values[:, n] - n * values[:, n - 1]) / (n + 1)
        slopes[:, n + 1] = slopes[:, n - 1] + (2 * n + 1) * values[:, n]
    return np.kron(values, values), np.kron(slopes, values), np.kron(values, slopes)


def face_points(face):
    t = np.arange(12)
    return (t, 132 + t, 12 * t, 12 * t + 11)[face]


def trace_table():
    _, xi, eta = legendre_tables()
    table = np.zeros((272, 144))
    table[np.arange(16), 128 + np.arange(16)] = 1.0
    for face in range(4):
        q = face_points(face)
        for at, rows in ((16, xi[q]), (80, eta[q]), (144, xi[q[::-1]]), (208, eta[q[::-1]])):
            table[at + 16 * face : at + 16 * face + 12] = rows
    return table


def point_table():
    basis, xi, eta = legendre_tables()
    return np.stack([np.concatenate([t[72 * h : 72 * h + 72] for t in (basis, xi, eta)]) for h in range(2)])


def half_face_rows(h):
    own = [(h, t) for t in range(1, 11)]
    along = range(1, 6) if h == 0 else range(6, 11)
    return own + [(f, t) for f in (2, 3) for t in along]


def pick_table():
    table = np.zeros((80, 128))
    for h in range(2):
        for g in range(2):
            for i, (f, t) in enumerate(half_face_rows(h)):
                table[40 * h + 20 * g + i, 64 * g + 16 * f + t] = 1.0
    return table


def place_table():
    table = np.zeros((2, 144, 40))
    for h in range(2):
        for g in range(2):
            for i, (f, t) in enumerate(half_face_rows(h)):
                table[h, 72 * g + face_points(f)[t] - 72 * h, 20 * g + i] = 1.0
    return table


def fourier_tables(planes, phys):
    m = np.arange(planes) // 2
    odd = np.arange(planes) % 2 == 1
    theta = (2.0 * np.pi / phys) * ((np.arange(phys)[None, :] * m[:, None]) % phys)
    weight = np.where(m == 0, 1.0, 2.0)[:, None]
    synth = np.where(odd[:, None], -weight * np.sin(theta), weight * np.cos(theta))
    analysis = np.where(odd[:, None], -np.sin(theta), np.cos(theta)) / phys
    return synth, analysis


def iota(shape, axis):
    return lax.broadcasted_iota(jnp.int32, shape, axis)


def to_element_rows():
    out, inp = iota((128, 128), 0), iota((128, 128), 1)
    return jnp.where(inp == ((out & 15) << 3) + (out >> 4), 1.0, 0.0).astype(BF16)


def reverse_faces():
    out, inp = iota((128, 128), 0), iota((128, 128), 1)
    t = out & 15
    return jnp.where((t < 12) & (inp == out - t + 11 - t), 1.0, 0.0).astype(BF16)


def dot(a, b):
    return jnp.dot(a, b, preferred_element_type=F32)


def dot_nt(a, b):
    return lax.dot_general(a, b, NT, preferred_element_type=F32)


def dot_tn(a, b):
    return lax.dot_general(a, b, (((0,), (0,)), ((), ())), preferred_element_type=F32)


def neighbours(blocks):
    me = lax.axis_index("elem")
    odd = lax.bitwise_and(me, 1)
    other = lax.bitwise_and(me + 2 * odd - 1 + blocks, blocks - 1)
    return me, (me + 1 - 2 * odd, other)


def start_copies(pairs, sems):
    copies = [pltpu.make_async_copy(src, dst, sems.at[i]) for i, (src, dst) in enumerate(pairs)]
    for copy in copies:
        copy.start()
    return copies


def average(own_ref, pick, element, places):
    tiles = [None] * 8
    for f in range(4):
        for g in range(2):
            own = own_ref[16 * element + 4 * g + f].astype(F32)
            other = own_ref[places[f] + 4 * g].astype(F32)
            tiles[4 * g + f] = (0.5 * (own + other)).astype(BF16)
    return dot(pick, jnp.concatenate(tiles, axis=0))


def pack_kernel(
    blocks, partner_hbm, side_hbm, flip_hbm, metric_hbm, v_hbm, table_hbm, pick_hbm, send_ref, own_ref, swap_ref_0, swap_ref_1, plan_ref,
    partner_ref, side_ref, flip_ref, metric_ref, v_ref, table_ref, pick_ref, rows_ref, place_ref, sems,
):
    copies = start_copies(
        (
            (v_hbm, v_ref),
            (table_hbm, table_ref),
            (partner_hbm, partner_ref),
            (metric_hbm, metric_ref),
            (side_hbm, side_ref),
            (flip_hbm, flip_ref),
            (pick_hbm, pick_ref),
        ),
        sems,
    )
    me, sides = neighbours(blocks)
    order = to_element_rows()
    rows_ref[:, 96:128, :] = jnp.zeros((8, 32, 144), BF16)
    for copy in copies:
        copy.wait()
    low, high, least = [jnp.int32(7)] * 2, [jnp.int32(0)] * 2, [jnp.int32(1 << 30)] * 2
    for e in range(8):
        for f in range(4):
            p = partner_ref[f, e]
            for i in range(2):
                there = lax.shift_right_arithmetic(p, 3) == sides[i]
                low[i] = jnp.where(there, jnp.minimum(low[i], e), low[i])
                high[i] = jnp.where(there, e, high[i])
                least[i] = jnp.where(there, jnp.minimum(least[i], p), least[i])
    table = table_ref[...]
    pick = pick_ref[...]
    for b in range(6):
        block = dot(order, v_ref[128 * b : 128 * b + 128, :]).astype(BF16)
        for e in range(8):
            rows_ref[e, 16 * b : 16 * b + 16, :] = block[16 * e : 16 * e + 16]
    for e in range(8):
        rows = rows_ref[e]
        out = dot_nt(table, rows)
        tail = out[0:16].astype(BF16)
        for h in range(2):
            send_ref[h, e, 0:96, :] = rows[0:96, 0:128]
            send_ref[h, e, 96:112, :] = tail
        for flip in range(2):
            xi = out[16 + 128 * flip : 80 + 128 * flip]
            eta = out[80 + 128 * flip : 144 + 128 * flip]
            for g in range(2):
                grad = xi * metric_ref[2 * g, e] + eta * metric_ref[2 * g + 1, e]
                at = 16 * e + 8 * flip + 4 * g
                own_ref[at : at + 4] = grad.astype(BF16).reshape(4, 16, 128)
    for i, out_ref in enumerate((swap_ref_0, swap_ref_1)):
        out_ref[0] = own_ref[pl.ds(16 * low[i], 8)]
        out_ref[1] = own_ref[pl.ds(16 * high[i], 8)]
    for e in range(8):
        places = []
        for f in range(4):
            p = partner_ref[f, e]
            home = lax.shift_right_arithmetic(p, 3)
            turn = flip_ref[f, e] * 8 + side_ref[f, e]
            near = lax.bitwise_and(p, 7) * 16 + turn
            far = jnp.where(home == sides[0], jnp.where(p == least[0], 128, 144), jnp.where(p == least[1], 160, 176)) + turn
            inside = jnp.where(home == me, near, 16 * e + f)
            place_ref[e, f] = jnp.where((p < 0) | (home == me), inside, far)
            places.append(inside)
        out = average(own_ref, pick, e, places)
        for h in range(2):
            send_ref[h, e, 112:152, :] = out[40 * h : 40 * h + 40].astype(BF16)
    for r, e in enumerate((low[0], high[0], low[1], high[1])):
        plan_ref[8 * r] = e
        for f in range(4):
            plan_ref[8 * r + 1 + f] = place_ref[e, f]


def border_kernel(plan_ref, swap_ref_0, swap_ref_1, pick_ref, own_in, send_in, own_ref, send_ref):
    reverse = reverse_faces()
    for k, ref in ((8, swap_ref_0), (10, swap_ref_1)):
        for i in range(2):
            at = 16 * (k + i)
            own_ref[at : at + 8] = ref[i]
            own_ref[at + 8 : at + 16] = dot(reverse, ref[i].reshape(128, 128)).astype(BF16).reshape(8, 16, 128)
    pick = pick_ref[...]
    for r in range(4):
        e = plan_ref[8 * r]
        out = average(own_ref, pick, e, [plan_ref[8 * r + 1 + f] for f in range(4)])
        for h in range(2):
            send_ref[h, e, 112:152, :] = out[40 * h : 40 * h + 40].astype(BF16)


def regroup(blocks):
    rows = blocks[0].shape[0]
    lane = iota((rows, 128), 1) >> 5
    out = []
    for c in range(3):
        groups = []
        for first in range(0, len(blocks), 4):
            group = None
            for k in range(4):
                shift = (32 * (k - c)) % 128
                piece = pltpu.roll(blocks[first + k], shift, 1) if shift else blocks[first + k]
                group = piece if group is None else jnp.where(lane == k, piece, group)
            groups.append(group)
        out.append(jnp.concatenate(groups, axis=1))
    return out


def main_kernel(metric_hbm, got_ref, table_ref, place_ref, synth_ref, analysis_ref, out_ref, field_ref, adv_ref, metric_ref, sems):
    (copy,) = start_copies(((metric_hbm, metric_ref),), sems)
    position = lax.axis_index("plane")
    elem, half = lax.bitwise_and(position, 7), lax.shift_right_logical(position, 3)
    table = table_ref[half]
    place = place_ref[half]
    tails = regroup([got_ref[p, 96:112, :].astype(F32) for p in range(16)])
    faces = regroup([got_ref[p, 112:152, :].astype(F32) for p in range(16)])
    on_face = dot(place, jnp.ones((40, 512), BF16)) > 0.5
    lane = iota((72, 128), 1)
    even = (lane & 1) == 0
    copy.wait()
    m = [metric_ref[k, elem] for k in range(4)]
    for c in range(3):
        modes = jnp.concatenate([got_ref[p, 32 * c : 32 * c + 32, :] for p in range(16)], axis=0)
        d = dot_nt(table[:, 0:128], modes) + dot(table[:, 128:144], tails[c].astype(BF16))
        value = d[0:72].astype(BF16).astype(F32)
        xi, eta = d[72:144], d[144:216]
        turned = []
        for g in range(4):
            v = value[:, 128 * g : 128 * g + 128]
            k = ((lane + 128 * g) >> 1).astype(F32) * (1.0 / 32.0)
            turned.append(jnp.where(even, -k * pltpu.roll(v, 127, 1), k * pltpu.roll(v, 1, 1)))
        field_ref[288 * c : 288 * c + 144, :] = jnp.concatenate([value, jnp.concatenate(turned, axis=1)], axis=0).astype(BF16)
        grads = jnp.concatenate([xi * m[0] + eta * m[1], xi * m[2] + eta * m[3]], axis=0)
        grads = jnp.where(on_face, dot(place, faces[c].astype(BF16)), grads)
        field_ref[288 * c + 144 : 288 * c + 288, :] = grads.astype(BF16)
    adv_ref[208:256, :] = jnp.zeros((48, 768), BF16)
    for j in range(0, 768, 256):
        phys = dot(field_ref[...], synth_ref[:, j : j + 256])
        terms = []
        for c in range(3):
            at = 288 * c
            terms.append(
                phys[0:72] * phys[at + 144 : at + 216]
                + phys[288:360] * phys[at + 216 : at + 288]
                + phys[576:648] * phys[at + 72 : at + 144]
            )
        terms.append(jnp.zeros((8, 256), F32))
        adv_ref[0:224, j : j + 256] = jnp.concatenate(terms, axis=0).astype(BF16)
    out = dot_nt(analysis_ref[...], adv_ref[...])
    out_ref[...] = out.astype(BF16).reshape(16, 32, 256)


def unpack_kernel(in_ref, out_hbm, out_ref, sems):
    out, inp = iota((128, 128), 0), iota((128, 128), 1)
    order = jnp.where(inp == ((out & 7) << 4) + (out >> 3), 1.0, 0.0).astype(BF16)
    lead, cols = iota((256, 144), 0) - iota((256, 144), 1), iota((256, 144), 1)
    mine = (cols < 72, cols >= 72)
    copies = []
    for c in range(3):
        block = None
        for z in range(2):
            pick = jnp.where((lead == 72 * (c - z)) & mine[z], 1.0, 0.0).astype(BF16)
            part = dot(in_ref[8 * z : 8 * z + 8].reshape(256, 256), pick)
            block = part if block is None else block + part
        block = block.astype(BF16)
        for b in range(2):
            piece = jnp.concatenate([block[32 * e + 16 * b : 32 * e + 16 * b + 16] for e in range(8)], axis=0)
            rows = pl.ds(256 * c + 128 * b, 128)
            out_ref[rows, :] = dot(order, piece).astype(BF16)
            copies.append(pltpu.make_async_copy(out_ref.at[rows], out_hbm.at[rows], sems.at[2 * c + b]))
            copies[-1].start()
    for copy in copies:
        copy.wait()


SMEM = pl.BlockSpec(memory_space=pltpu.SMEM)
VMEM = pl.BlockSpec(memory_space=pltpu.VMEM)
HBM = pl.BlockSpec(memory_space=pltpu.HBM)


def call(kernel, in_specs, out_shapes, scratch=(), aliases=None, out_specs=None):
    single = not isinstance(out_shapes, (list, tuple)) or hasattr(out_shapes, "shape")
    return pl.pallas_call(
        kernel,
        in_specs=in_specs,
        out_specs=out_specs or (VMEM if single else [VMEM] * len(out_shapes)),
        out_shape=out_shapes,
        scratch_shapes=list(scratch),
        compiler_params=pltpu.CompilerParams(vmem_limit_bytes=40 * 1024 * 1024),
        input_output_aliases=aliases or {},
        interpret=INTERPRET,
    )


def in_hbm(x):
    return x if INTERPRET else pltpu.with_memory_space_constraint(x, pltpu.HBM)


def shape(*dims):
    return jax.ShapeDtypeStruct(dims, BF16)


def on_device(velocity_modes, metric, face_partner, face_side, face_flip):
    blocks = lax.axis_size("elem")
    within = [(i, i ^ 1) for i in range(blocks)]
    across = [((i + 1) % blocks, ((i ^ 1) + 1) % blocks) for i in range(blocks)]
    synth, analysis = fourier_tables(512, 768)
    pick, geometry = bf16(pick_table()), in_hbm(metric.T)
    send, own, to_first, to_second, plan = call(
        functools.partial(pack_kernel, blocks),
        [HBM] * 7,
        [
            shape(2, 8, 152, 128),
            shape(192, 16, 128),
            shape(2, 8, 16, 128),
            shape(2, 8, 16, 128),
            jax.ShapeDtypeStruct((32,), jnp.int32),
        ],
        [
            pltpu.SMEM((4, 8), jnp.int32),
            pltpu.SMEM((4, 8), jnp.int32),
            pltpu.SMEM((4, 8), jnp.int32),
            pltpu.SMEM((4, 8), F32),
            pltpu.VMEM((768, 144), BF16),
            pltpu.VMEM((272, 144), BF16),
            pltpu.VMEM((80, 128), BF16),
            pltpu.VMEM((8, 128, 144), BF16),
            pltpu.SMEM((8, 4), jnp.int32),
            pltpu.SemaphoreType.DMA((7,)),
        ],
        out_specs=[VMEM] * 4 + [SMEM],
    )(
        in_hbm(face_partner.T),
        in_hbm(face_side.T),
        in_hbm(face_flip.T),
        geometry,
        in_hbm(velocity_modes.reshape(768, 144)),
        in_hbm(bf16(trace_table())),
        in_hbm(pick),
    )
    from_first = lax.ppermute(to_first, "elem", within)
    from_second = lax.ppermute(to_second, "elem", across)
    _, send = call(
        border_kernel,
        [SMEM, VMEM, VMEM, VMEM, VMEM, VMEM],
        [shape(192, 16, 128), shape(2, 8, 152, 128)],
        aliases={4: 0, 5: 1},
    )(plan, from_first, from_second, pick, own, send)
    got = lax.all_to_all(send.reshape(16, 152, 128), "plane", 0, 0, tiled=True)
    out = call(
        main_kernel,
        [HBM, VMEM, VMEM, VMEM, VMEM, VMEM],
        shape(16, 32, 256),
        [
            pltpu.VMEM((864, 512), BF16),
            pltpu.VMEM((256, 768), BF16),
            pltpu.SMEM((4, 8), F32),
            pltpu.SemaphoreType.DMA((1,)),
        ],
    )(geometry, got, bf16(point_table()), bf16(place_table()), bf16(synth), bf16(analysis))
    out = lax.all_to_all(out, "plane", 0, 0, tiled=True)
    out = call(
        unpack_kernel,
        [VMEM],
        shape(768, 144),
        [pltpu.VMEM((768, 144), BF16), pltpu.SemaphoreType.DMA((6,))],
        out_specs=HBM,
    )(out)
    return out.reshape(3, 32, 8, 144)


def solution(mesh):
    by_elem = P("elem", None)
    whole = P(None, "plane", "elem", None)
    return jax.shard_map(
        on_device,
        mesh=mesh,
        in_specs=(whole, by_elem, by_elem, by_elem, by_elem),
        out_specs=whole,
        check_vma=False,
    )
```

```python
import functools

import jax
import jax.numpy as jnp
import numpy as np
from jax import lax
from jax.experimental import pallas as pl
from jax.experimental.pallas import tpu as pltpu
from jax.sharding import PartitionSpec as P

F32, BF16 = jnp.float32, jnp.bfloat16
NT = (((1,), (1,)), ((), ()))
INTERPRET = False


def bf16(table):
    return jnp.asarray(np.asarray(table, np.float32)).astype(BF16)


def legendre_tables():
    points = -np.cos(np.pi * np.arange(12) / 11.0)
    values, slopes = np.zeros((12, 12)), np.zeros((12, 12))
    values[:, 0] = 1.0
    values[:, 1] = points
    slopes[:, 1] = 1.0
    for n in range(1, 11):
        values[:, n + 1] = ((2 * n + 1) * points * values[:, n] - n * values[:, n - 1]) / (n + 1)
        slopes[:, n + 1] = slopes[:, n - 1] + (2 * n + 1) * values[:, n]
    return np.kron(values, values), np.kron(slopes, values), np.kron(values, slopes)


def face_points(face):
    t = np.arange(12)
    return (t, 132 + t, 12 * t, 12 * t + 11)[face]


def trace_table():
    _, xi, eta = legendre_tables()
    table = np.zeros((272, 144))
    table[np.arange(16), 128 + np.arange(16)] = 1.0
    for face in range(4):
        q = face_points(face)
        for at, rows in ((16, xi[q]), (80, eta[q]), (144, xi[q[::-1]]), (208, eta[q[::-1]])):
            table[at + 16 * face : at + 16 * face + 12] = rows
    return table


def point_table():
    basis, xi, eta = legendre_tables()
    return np.stack([np.concatenate([t[72 * h : 72 * h + 72] for t in (basis, xi, eta)]) for h in range(2)])


def half_face_rows(h):
    own = [(h, t) for t in range(1, 11)]
    along = range(1, 6) if h == 0 else range(6, 11)
    return own + [(f, t) for f in (2, 3) for t in along]


def pick_table():
    table = np.zeros((80, 128))
    for h in range(2):
        for g in range(2):
            for i, (f, t) in enumerate(half_face_rows(h)):
                table[40 * h + 20 * g + i, 64 * g + 16 * f + t] = 1.0
    return table


def place_table():
    table = np.zeros((2, 144, 40))
    for h in range(2):
        for g in range(2):
            for i, (f, t) in enumerate(half_face_rows(h)):
                table[h, 72 * g + face_points(f)[t] - 72 * h, 20 * g + i] = 1.0
    return table


def fourier_tables(planes, phys):
    m = np.arange(planes) // 2
    odd = np.arange(planes) % 2 == 1
    theta = (2.0 * np.pi / phys) * ((np.arange(phys)[None, :] * m[:, None]) % phys)
    weight = np.where(m == 0, 1.0, 2.0)[:, None]
    synth = np.where(odd[:, None], -weight * np.sin(theta), weight * np.cos(theta))
    analysis = np.where(odd[:, None], -np.sin(theta), np.cos(theta)) / phys
    return synth, analysis


def iota(shape, axis):
    return lax.broadcasted_iota(jnp.int32, shape, axis)


def to_element_rows():
    out, inp = iota((128, 128), 0), iota((128, 128), 1)
    return jnp.where(inp == ((out & 15) << 3) + (out >> 4), 1.0, 0.0).astype(BF16)


def reverse_faces():
    out, inp = iota((128, 128), 0), iota((128, 128), 1)
    t = out & 15
    return jnp.where((t < 12) & (inp == out - t + 11 - t), 1.0, 0.0).astype(BF16)


def dot(a, b):
    return jnp.dot(a, b, preferred_element_type=F32)


def dot_nt(a, b):
    return lax.dot_general(a, b, NT, preferred_element_type=F32)


def dot_tn(a, b):
    return lax.dot_general(a, b, (((0,), (0,)), ((), ())), preferred_element_type=F32)


def neighbours(blocks):
    me = lax.axis_index("elem")
    return me, (lax.bitwise_and(me + blocks - 1, blocks - 1), lax.bitwise_and(me + 1, blocks - 1))


def start_copies(pairs, sems):
    copies = [pltpu.make_async_copy(src, dst, sems.at[i]) for i, (src, dst) in enumerate(pairs)]
    for copy in copies:
        copy.start()
    return copies


def average(own_ref, pick, element, places):
    tiles = [None] * 8
    for f in range(4):
        for g in range(2):
            own = own_ref[16 * element + 4 * g + f].astype(F32)
            other = own_ref[places[f] + 4 * g].astype(F32)
            tiles[4 * g + f] = (0.5 * (own + other)).astype(BF16)
    return dot(pick, jnp.concatenate(tiles, axis=0))


def everywhere(reduce, x):
    return reduce(reduce(x, axis=1, keepdims=True), axis=0, keepdims=True)


def pack_kernel(
    blocks, partner_hbm, side_hbm, flip_hbm, metric_hbm, v_hbm, table_hbm, pick_hbm, send_ref, own_ref, prev_ref, next_ref, plan_ref,
    partner_ref, side_ref, flip_ref, metric_ref, v_ref, table_ref, pick_ref, rows_ref, place_ref, sems,
):
    copies = start_copies(
        (
            (v_hbm, v_ref),
            (table_hbm, table_ref),
            (partner_hbm, partner_ref),
            (metric_hbm, metric_ref),
            (side_hbm, side_ref),
            (flip_hbm, flip_ref),
            (pick_hbm, pick_ref),
        ),
        sems,
    )
    me, sides = neighbours(blocks)
    order = to_element_rows()
    rows_ref[:, 96:128, :] = jnp.zeros((8, 32, 144), BF16)
    for copy in copies:
        copy.wait()
    p = partner_ref[...]
    home = p >> 3
    e, f = iota((4, 8), 1).astype(F32), iota((4, 8), 0).astype(F32)
    number = p.astype(F32)
    turn = (flip_ref[...] * 8 + side_ref[...]).astype(F32)
    there = [home == side for side in sides]
    low = [everywhere(jnp.min, jnp.where(t, e, 7.0)) for t in there]
    high = [everywhere(jnp.max, jnp.where(t, e, 0.0)) for t in there]
    least = [everywhere(jnp.min, jnp.where(t, number, 1e9)) for t in there]
    near = ((p & 7) << 4).astype(F32) + turn
    inside = jnp.where(home == me, near, 16.0 * e + f)
    first = jnp.where(number == least[0], 128.0, 144.0) + turn
    second = jnp.where(number == least[1], 160.0, 176.0) + turn
    plan_ref[0:4, 0:8] = inside.astype(jnp.int32)
    plan_ref[4:8, 0:8] = jnp.where(there[0], first, jnp.where(there[1], second, inside)).astype(jnp.int32)
    column = iota((1, 8), 1)
    ends = jnp.where(column == 0, low[0], jnp.where(column == 1, high[0], jnp.where(column == 2, low[1], high[1])))
    plan_ref[8:9, 0:8] = ends.astype(jnp.int32)
    (plan_copy,) = start_copies(((plan_ref, place_ref),), sems)
    table = table_ref[...]
    pick = pick_ref[...]
    for b in range(6):
        block = dot(order, v_ref[128 * b : 128 * b + 128, :]).astype(BF16)
        for e in range(8):
            rows_ref[e, 16 * b : 16 * b + 16, :] = block[16 * e : 16 * e + 16]
    for e in range(8):
        rows = rows_ref[e]
        out = dot_nt(table, rows)
        tail = out[0:16].astype(BF16)
        for h in range(2):
            send_ref[h, e, 0:96, :] = rows[0:96, 0:128]
            send_ref[h, e, 96:112, :] = tail
        for flip in range(2):
            xi = out[16 + 128 * flip : 80 + 128 * flip]
            eta = out[80 + 128 * flip : 144 + 128 * flip]
            for g in range(2):
                grad = xi * metric_ref[2 * g, e] + eta * metric_ref[2 * g + 1, e]
                at = 16 * e + 8 * flip + 4 * g
                own_ref[at : at + 4] = grad.astype(BF16).reshape(4, 16, 128)
    plan_copy.wait()
    for i, out_ref in enumerate((prev_ref, next_ref)):
        for k in range(2):
            out_ref[k] = own_ref[pl.ds(16 * place_ref[8, 2 * i + k], 8)]
    for e in range(8):
        out = average(own_ref, pick, e, [place_ref[f, e] for f in range(4)])
        for h in range(2):
            send_ref[h, e, 112:152, :] = out[40 * h : 40 * h + 40].astype(BF16)


def border_kernel(plan_ref, prev_ref, next_ref, pick_ref, own_in, send_in, own_ref, send_ref):
    reverse = reverse_faces()
    for k, ref in ((8, prev_ref), (10, next_ref)):
        for i in range(2):
            at = 16 * (k + i)
            own_ref[at : at + 8] = ref[i]
            own_ref[at + 8 : at + 16] = dot(reverse, ref[i].reshape(128, 128)).astype(BF16).reshape(8, 16, 128)
    pick = pick_ref[...]
    for r in range(4):
        e = plan_ref[8, r]
        out = average(own_ref, pick, e, [plan_ref[4 + f, e] for f in range(4)])
        for h in range(2):
            send_ref[h, e, 112:152, :] = out[40 * h : 40 * h + 40].astype(BF16)


def regroup(blocks):
    rows = blocks[0].shape[0]
    lane = iota((rows, 128), 1) >> 5
    out = []
    for c in range(3):
        groups = []
        for first in range(0, len(blocks), 4):
            group = None
            for k in range(4):
                shift = (32 * (k - c)) % 128
                piece = pltpu.roll(blocks[first + k], shift, 1) if shift else blocks[first + k]
                group = piece if group is None else jnp.where(lane == k, piece, group)
            groups.append(group)
        out.append(jnp.concatenate(groups, axis=1))
    return out


def main_kernel(metric_hbm, got_ref, table_ref, place_ref, synth_ref, analysis_ref, out_ref, field_ref, adv_ref, metric_ref, sems):
    (copy,) = start_copies(((metric_hbm, metric_ref),), sems)
    position = lax.axis_index("plane")
    elem, half = lax.bitwise_and(position, 7), lax.shift_right_logical(position, 3)
    table = table_ref[half]
    place = place_ref[half]
    tails = regroup([got_ref[p, 96:112, :].astype(F32) for p in range(16)])
    faces = regroup([got_ref[p, 112:152, :].astype(F32) for p in range(16)])
    on_face = dot(place, jnp.ones((40, 128), BF16)) > 0.5
    lane = iota((72, 128), 1)
    even = (lane & 1) == 0
    copy.wait()
    m = [metric_ref[k, elem] for k in range(4)]
    for c in range(3):
        modes = jnp.concatenate([got_ref[p, 32 * c : 32 * c + 32, :] for p in range(16)], axis=0)
        d = dot_nt(table[:, 0:128], modes) + dot(table[:, 128:144], tails[c].astype(BF16))
        value = d[0:72].astype(BF16).astype(F32)
        xi, eta = d[72:144], d[144:216]
        turned = []
        for g in range(4):
            v = value[:, 128 * g : 128 * g + 128]
            k = ((lane + 128 * g) >> 1).astype(F32) * (1.0 / 32.0)
            turned.append(jnp.where(even, -k * pltpu.roll(v, 127, 1), k * pltpu.roll(v, 1, 1)))
        field_ref[288 * c : 288 * c + 144, :] = jnp.concatenate([value, jnp.concatenate(turned, axis=1)], axis=0).astype(BF16)
        grads = jnp.concatenate([xi * m[0] + eta * m[1], xi * m[2] + eta * m[3]], axis=0)
        at_faces = dot(place, faces[c].astype(BF16))
        grads = jnp.concatenate(
            [jnp.where(on_face, at_faces[:, at : at + 128], grads[:, at : at + 128]) for at in range(0, 512, 128)], axis=1
        )
        field_ref[288 * c + 144 : 288 * c + 288, :] = grads.astype(BF16)
    adv_ref[208:256, :] = jnp.zeros((48, 768), BF16)
    for j in range(0, 768, 256):
        phys = dot(field_ref[...], synth_ref[:, j : j + 256])
        terms = []
        for c in range(3):
            at = 288 * c
            terms.append(
                phys[0:72] * phys[at + 144 : at + 216]
                + phys[288:360] * phys[at + 216 : at + 288]
                + phys[576:648] * phys[at + 72 : at + 144]
            )
        terms.append(jnp.zeros((8, 256), F32))
        adv_ref[0:224, j : j + 256] = jnp.concatenate(terms, axis=0).astype(BF16)
    out = dot_nt(analysis_ref[...], adv_ref[...])
    out_ref[...] = out.astype(BF16).reshape(16, 32, 256)


def unpack_kernel(in_ref, out_hbm, out_ref, sems):
    out, inp = iota((128, 128), 0), iota((128, 128), 1)
    order = jnp.where(inp == ((out & 7) << 4) + (out >> 3), 1.0, 0.0).astype(BF16)
    lane = iota((128, 128), 1)
    left = lane < 72
    copies = []
    for b in range(2):
        halves = []
        for z in range(2):
            piece = jnp.concatenate([in_ref[8 * z + e, 16 * b : 16 * b + 16, :] for e in range(8)], axis=0)
            halves.append(dot(order, piece))
        a0, a1 = halves[0][:, 0:128], halves[0][:, 128:256]
        b0, b1 = halves[1][:, 0:128], halves[1][:, 128:256]
        for c in range(3):
            if c == 0:
                upper = pltpu.roll(b0, 72, 1)
                first, second = jnp.where(left, a0, upper), upper
            elif c == 1:
                lower = jnp.where(lane < 56, pltpu.roll(a0, 56, 1), pltpu.roll(a1, 56, 1))
                first, second = jnp.where(left, lower, b0), b1
            else:
                upper = pltpu.roll(b1, 56, 1)
                first, second = jnp.where(left, pltpu.roll(a1, 112, 1), upper), upper
            rows = pl.ds(256 * c + 128 * b, 128)
            out_ref[rows, 0:128] = first.astype(BF16)
            out_ref[rows, 128:144] = second[:, 0:16].astype(BF16)
            copies.append(pltpu.make_async_copy(out_ref.at[rows], out_hbm.at[rows], sems.at[2 * c + b]))
            copies[-1].start()
    for copy in copies:
        copy.wait()


SMEM = pl.BlockSpec(memory_space=pltpu.SMEM)
VMEM = pl.BlockSpec(memory_space=pltpu.VMEM)
HBM = pl.BlockSpec(memory_space=pltpu.HBM)


def call(kernel, in_specs, out_shapes, scratch=(), aliases=None, out_specs=None):
    single = not isinstance(out_shapes, (list, tuple)) or hasattr(out_shapes, "shape")
    return pl.pallas_call(
        kernel,
        in_specs=in_specs,
        out_specs=out_specs or (VMEM if single else [VMEM] * len(out_shapes)),
        out_shape=out_shapes,
        scratch_shapes=list(scratch),
        compiler_params=pltpu.CompilerParams(vmem_limit_bytes=40 * 1024 * 1024),
        input_output_aliases=aliases or {},
        interpret=INTERPRET,
    )


def in_hbm(x):
    return x if INTERPRET else pltpu.with_memory_space_constraint(x, pltpu.HBM)


def shape(*dims):
    return jax.ShapeDtypeStruct(dims, BF16)


def on_device(velocity_modes, metric, face_partner, face_side, face_flip):
    blocks = lax.axis_size("elem")
    up = [(i, (i + 1) % blocks) for i in range(blocks)]
    down = [(j, i) for i, j in up]
    synth, analysis = fourier_tables(512, 768)
    pick, geometry = bf16(pick_table()), in_hbm(metric.T)
    send, own, to_prev, to_next, plan = call(
        functools.partial(pack_kernel, blocks),
        [HBM] * 7,
        [
            shape(2, 8, 152, 128),
            shape(192, 16, 128),
            shape(2, 8, 16, 128),
            shape(2, 8, 16, 128),
            jax.ShapeDtypeStruct((16, 128), jnp.int32),
        ],
        [
            pltpu.VMEM((4, 8), jnp.int32),
            pltpu.VMEM((4, 8), jnp.int32),
            pltpu.VMEM((4, 8), jnp.int32),
            pltpu.SMEM((4, 8), F32),
            pltpu.VMEM((768, 144), BF16),
            pltpu.VMEM((272, 144), BF16),
            pltpu.VMEM((80, 128), BF16),
            pltpu.VMEM((8, 128, 144), BF16),
            pltpu.SMEM((16, 128), jnp.int32),
            pltpu.SemaphoreType.DMA((7,)),
        ],
        out_specs=[VMEM] * 5,
    )(
        in_hbm(face_partner.T),
        in_hbm(face_side.T),
        in_hbm(face_flip.T),
        geometry,
        in_hbm(velocity_modes.reshape(768, 144)),
        in_hbm(bf16(trace_table())),
        in_hbm(pick),
    )
    from_prev = lax.ppermute(to_next, "elem", up)
    from_next = lax.ppermute(to_prev, "elem", down)
    _, send = call(
        border_kernel,
        [SMEM, VMEM, VMEM, VMEM, VMEM, VMEM],
        [shape(192, 16, 128), shape(2, 8, 152, 128)],
        aliases={4: 0, 5: 1},
    )(plan, from_prev, from_next, pick, own, send)
    got = lax.all_to_all(send.reshape(16, 152, 128), "plane", 0, 0, tiled=True)
    out = call(
        main_kernel,
        [HBM, VMEM, VMEM, VMEM, VMEM, VMEM],
        shape(16, 32, 256),
        [
            pltpu.VMEM((864, 512), BF16),
            pltpu.VMEM((256, 768), BF16),
            pltpu.SMEM((4, 8), F32),
            pltpu.SemaphoreType.DMA((1,)),
        ],
    )(geometry, got, bf16(point_table()), bf16(place_table()), bf16(synth), bf16(analysis))
    out = lax.all_to_all(out, "plane", 0, 0, tiled=True)
    out = call(
        unpack_kernel,
        [VMEM],
        shape(768, 144),
        [pltpu.VMEM((768, 144), BF16), pltpu.SemaphoreType.DMA((6,))],
        out_specs=HBM,
    )(out)
    return out.reshape(3, 32, 8, 144)


def solution(mesh):
    by_elem = P("elem", None)
    whole = P(None, "plane", "elem", None)
    return jax.shard_map(
        on_device,
        mesh=mesh,
        in_specs=(whole, by_elem, by_elem, by_elem, by_elem),
        out_specs=whole,
        check_vma=False,
    )
```

```python
import functools

import jax
import jax.numpy as jnp
import numpy as np
from jax import lax
from jax.experimental import pallas as pl
from jax.experimental.pallas import tpu as pltpu
from jax.sharding import PartitionSpec as P

F32, BF16 = jnp.float32, jnp.bfloat16
NT = (((1,), (1,)), ((), ()))
INTERPRET = False


def bf16(table):
    return jnp.asarray(np.asarray(table, np.float32)).astype(BF16)


def legendre_tables():
    points = -np.cos(np.pi * np.arange(12) / 11.0)
    values, slopes = np.zeros((12, 12)), np.zeros((12, 12))
    values[:, 0] = 1.0
    values[:, 1] = points
    slopes[:, 1] = 1.0
    for n in range(1, 11):
        values[:, n + 1] = ((2 * n + 1) * points * values[:, n] - n * values[:, n - 1]) / (n + 1)
        slopes[:, n + 1] = slopes[:, n - 1] + (2 * n + 1) * values[:, n]
    return np.kron(values, values), np.kron(slopes, values), np.kron(values, slopes)


def face_points(face):
    t = np.arange(12)
    return (t, 132 + t, 12 * t, 12 * t + 11)[face]


def trace_table():
    _, xi, eta = legendre_tables()
    table = np.zeros((272, 144))
    table[np.arange(16), 128 + np.arange(16)] = 1.0
    for face in range(4):
        q = face_points(face)
        for at, rows in ((16, xi[q]), (80, eta[q]), (144, xi[q[::-1]]), (208, eta[q[::-1]])):
            table[at + 16 * face : at + 16 * face + 12] = rows
    return table


def point_table():
    basis, xi, eta = legendre_tables()
    return np.stack([np.concatenate([t[72 * h : 72 * h + 72] for t in (basis, xi, eta)]) for h in range(2)])


def half_face_rows(h):
    own = [(h, t) for t in range(1, 11)]
    along = range(1, 6) if h == 0 else range(6, 11)
    return own + [(f, t) for f in (2, 3) for t in along]


def pick_table():
    table = np.zeros((80, 128))
    for h in range(2):
        for g in range(2):
            for i, (f, t) in enumerate(half_face_rows(h)):
                table[40 * h + 20 * g + i, 64 * g + 16 * f + t] = 1.0
    return table


def place_table():
    table = np.zeros((2, 144, 40))
    for h in range(2):
        for g in range(2):
            for i, (f, t) in enumerate(half_face_rows(h)):
                table[h, 72 * g + face_points(f)[t] - 72 * h, 20 * g + i] = 1.0
    return table


def fourier_tables(planes, phys):
    m = np.arange(planes) // 2
    odd = np.arange(planes) % 2 == 1
    theta = (2.0 * np.pi / phys) * ((np.arange(phys)[None, :] * m[:, None]) % phys)
    weight = np.where(m == 0, 1.0, 2.0)[:, None]
    synth = np.where(odd[:, None], -weight * np.sin(theta), weight * np.cos(theta))
    analysis = np.where(odd[:, None], -np.sin(theta), np.cos(theta)) / phys
    return synth, analysis


def iota(shape, axis):
    return lax.broadcasted_iota(jnp.int32, shape, axis)


def to_element_rows():
    out, inp = iota((128, 128), 0), iota((128, 128), 1)
    return jnp.where(inp == ((out & 15) << 3) + (out >> 4), 1.0, 0.0).astype(BF16)


def reverse_faces():
    out, inp = iota((128, 128), 0), iota((128, 128), 1)
    t = out & 15
    return jnp.where((t < 12) & (inp == out - t + 11 - t), 1.0, 0.0).astype(BF16)


def dot(a, b):
    return jnp.dot(a, b, preferred_element_type=F32)


def dot_nt(a, b):
    return lax.dot_general(a, b, NT, preferred_element_type=F32)


def dot_tn(a, b):
    return lax.dot_general(a, b, (((0,), (0,)), ((), ())), preferred_element_type=F32)


def neighbours(blocks):
    me = lax.axis_index("elem")
    return me, (lax.bitwise_and(me + blocks - 1, blocks - 1), lax.bitwise_and(me + 1, blocks - 1))


def start_copies(pairs, sems):
    copies = [pltpu.make_async_copy(src, dst, sems.at[i]) for i, (src, dst) in enumerate(pairs)]
    for copy in copies:
        copy.start()
    return copies


def average(own_ref, pick, element, places):
    tiles = [None] * 8
    for f in range(4):
        for g in range(2):
            own = own_ref[16 * element + 4 * g + f].astype(F32)
            other = own_ref[places[f] + 4 * g].astype(F32)
            tiles[4 * g + f] = (0.5 * (own + other)).astype(BF16)
    return dot(pick, jnp.concatenate(tiles, axis=0))


def everywhere(reduce, x):
    return reduce(reduce(x, axis=1, keepdims=True), axis=0, keepdims=True)


def pack_kernel(
    blocks, partner_hbm, side_hbm, flip_hbm, metric_hbm, v_hbm, table_hbm, pick_hbm, send_ref, own_ref, prev_ref, next_ref, plan_ref,
    partner_ref, side_ref, flip_ref, metric_ref, v_ref, table_ref, pick_ref, rows_ref, tail_ref, place_ref, sems,
):
    parts = [pl.ds(256 * i, 256) for i in range(3)]
    copies = start_copies(
        [(v_hbm.at[part], v_ref.at[part]) for part in parts]
        + [
            (table_hbm, table_ref),
            (partner_hbm, partner_ref),
            (metric_hbm, metric_ref),
            (side_hbm, side_ref),
            (flip_hbm, flip_ref),
            (pick_hbm, pick_ref),
        ],
        sems,
    )
    me, sides = neighbours(blocks)
    order = to_element_rows()
    rows_ref[:, 96:128, :] = jnp.zeros((8, 32, 144), BF16)
    for b in range(6):
        if b % 2 == 0:
            copies[b // 2].wait()
        block = dot(order, v_ref[128 * b : 128 * b + 128, :]).astype(BF16)
        for e in range(8):
            rows_ref[e, 16 * b : 16 * b + 16, :] = block[16 * e : 16 * e + 16]
    for copy in copies[3:]:
        copy.wait()
    p = partner_ref[...]
    home = p >> 3
    e, f = iota((4, 8), 1).astype(F32), iota((4, 8), 0).astype(F32)
    number = p.astype(F32)
    turn = (flip_ref[...] * 8 + side_ref[...]).astype(F32)
    there = [home == side for side in sides]
    low = [everywhere(jnp.min, jnp.where(t, e, 7.0)) for t in there]
    high = [everywhere(jnp.max, jnp.where(t, e, 0.0)) for t in there]
    least = [everywhere(jnp.min, jnp.where(t, number, 1e9)) for t in there]
    near = ((p & 7) << 4).astype(F32) + turn
    inside = jnp.where(home == me, near, 16.0 * e + f)
    first = jnp.where(number == least[0], 128.0, 144.0) + turn
    second = jnp.where(number == least[1], 160.0, 176.0) + turn
    plan_ref[0:4, 0:8] = inside.astype(jnp.int32)
    plan_ref[4:8, 0:8] = jnp.where(there[0], first, jnp.where(there[1], second, inside)).astype(jnp.int32)
    column = iota((1, 8), 1)
    ends = jnp.where(column == 0, low[0], jnp.where(column == 1, high[0], jnp.where(column == 2, low[1], high[1])))
    plan_ref[8:9, 0:8] = ends.astype(jnp.int32)
    (plan_copy,) = start_copies(((plan_ref, place_ref),), sems)
    table = table_ref[...]
    pick = pick_ref[...]
    for e in range(8):
        rows = rows_ref[e]
        out = dot_nt(table, rows)
        tail_ref[e] = out[0:16]
        for h in range(2):
            send_ref[h, e, 0:96, :] = rows[0:96, 0:128]
        for flip in range(2):
            xi = out[16 + 128 * flip : 80 + 128 * flip]
            eta = out[80 + 128 * flip : 144 + 128 * flip]
            for g in range(2):
                grad = xi * metric_ref[2 * g, e] + eta * metric_ref[2 * g + 1, e]
                at = 16 * e + 8 * flip + 4 * g
                own_ref[at : at + 4] = grad.astype(BF16).reshape(4, 16, 128)
    plan_copy.wait()
    taken = iota((40, 128), 1) < 96
    for i, out_ref in enumerate((prev_ref, next_ref)):
        for k in range(2):
            out_ref[k] = own_ref[pl.ds(16 * place_ref[8, 2 * i + k], 8)]
    for e in range(8):
        out = average(own_ref, pick, e, [place_ref[f, e] for f in range(4)])
        upper = tail_ref[e, 8:16]
        spare = jnp.concatenate([pltpu.roll(upper, 96 - 32 * c, 1) for c in range(3)] + [jnp.zeros((16, 128), F32)], axis=0)
        for h in range(2):
            face = jnp.where(taken, out[40 * h : 40 * h + 40], spare)
            send_ref[h, e, 96:144, :] = jnp.concatenate([tail_ref[e, 0:8], face], axis=0).astype(BF16)


def border_kernel(plan_ref, prev_ref, next_ref, pick_ref, own_in, send_in, own_ref, send_ref, place_ref, sems):
    (plan_copy,) = start_copies(((plan_ref, place_ref),), sems)
    reverse = reverse_faces()
    for k, ref in ((8, prev_ref), (10, next_ref)):
        for i in range(2):
            at = 16 * (k + i)
            own_ref[at : at + 8] = ref[i]
            own_ref[at + 8 : at + 16] = dot(reverse, ref[i].reshape(128, 128)).astype(BF16).reshape(8, 16, 128)
    pick = pick_ref[...]
    row, lane = iota((48, 128), 0), iota((48, 128), 1)
    kept = (row < 8) | (lane >= 96)
    plan_copy.wait()
    for r in range(4):
        e = place_ref[8, r]
        out = average(own_ref, pick, e, [place_ref[4 + f, e] for f in range(4)])
        for h in range(2):
            old = send_ref[h, e, 96:144, :].astype(F32)
            face = jnp.concatenate([jnp.zeros((8, 128), F32), out[40 * h : 40 * h + 40]], axis=0)
            send_ref[h, e, 96:144, :] = jnp.where(kept, old, face).astype(BF16)


def regroup(blocks, lanes=(0, 32, 64)):
    rows = blocks[0].shape[0]
    lane = iota((rows, 128), 1) >> 5
    out = []
    for start in lanes:
        groups = []
        for first in range(0, len(blocks), 4):
            group = None
            for k in range(4):
                shift = (32 * k - start) % 128
                piece = pltpu.roll(blocks[first + k], shift, 1) if shift else blocks[first + k]
                group = piece if group is None else jnp.where(lane == k, piece, group)
            groups.append(group)
        out.append(jnp.concatenate(groups, axis=1))
    return out


def main_kernel(metric_hbm, got_ref, table_ref, place_ref, synth_ref, analysis_ref, out_ref, field_ref, adv_ref, metric_ref, sems):
    (copy,) = start_copies(((metric_hbm, metric_ref),), sems)
    position = lax.axis_index("plane")
    elem, half = lax.bitwise_and(position, 7), lax.shift_right_logical(position, 3)
    table = table_ref[half]
    place = place_ref[half]
    blocks = [got_ref[p, 96:144, :].astype(F32) for p in range(16)]
    lower = regroup([block[0:8] for block in blocks])
    upper = [regroup([block[8 * c + 8 : 8 * c + 16] for block in blocks], (96,))[0] for c in range(3)]
    tails = [jnp.concatenate([lower[c], upper[c]], axis=0) for c in range(3)]
    faces = regroup([block[8:48] for block in blocks])
    on_face = dot(place, jnp.ones((40, 128), BF16)) > 0.5
    lane = iota((72, 128), 1)
    even = (lane & 1) == 0
    copy.wait()
    m = [metric_ref[k, elem] for k in range(4)]
    for c in range(3):
        modes = jnp.concatenate([got_ref[p, 32 * c : 32 * c + 32, :] for p in range(16)], axis=0)
        d = dot_nt(table[:, 0:128], modes) + dot(table[:, 128:144], tails[c].astype(BF16))
        value = d[0:72].astype(BF16).astype(F32)
        xi, eta = d[72:144], d[144:216]
        turned = []
        for g in range(4):
            v = value[:, 128 * g : 128 * g + 128]
            k = ((lane + 128 * g) >> 1).astype(F32) * (1.0 / 32.0)
            turned.append(jnp.where(even, -k * pltpu.roll(v, 127, 1), k * pltpu.roll(v, 1, 1)))
        field_ref[288 * c : 288 * c + 144, :] = jnp.concatenate([value, jnp.concatenate(turned, axis=1)], axis=0).astype(BF16)
        grads = jnp.concatenate([xi * m[0] + eta * m[1], xi * m[2] + eta * m[3]], axis=0)
        at_faces = dot(place, faces[c].astype(BF16))
        grads = jnp.concatenate(
            [jnp.where(on_face, at_faces[:, at : at + 128], grads[:, at : at + 128]) for at in range(0, 512, 128)], axis=1
        )
        field_ref[288 * c + 144 : 288 * c + 288, :] = grads.astype(BF16)
    adv_ref[208:256, :] = jnp.zeros((48, 768), BF16)
    for j in range(0, 768, 256):
        phys = dot(field_ref[...], synth_ref[:, j : j + 256])
        terms = []
        for c in range(3):
            at = 288 * c
            terms.append(
                phys[0:72] * phys[at + 144 : at + 216]
                + phys[288:360] * phys[at + 216 : at + 288]
                + phys[576:648] * phys[at + 72 : at + 144]
            )
        terms.append(jnp.zeros((8, 256), F32))
        adv_ref[0:224, j : j + 256] = jnp.concatenate(terms, axis=0).astype(BF16)
    out = dot_nt(analysis_ref[...], adv_ref[...])
    left = iota((8, 128), 1) < 88
    for p in range(16):
        out_ref[p, 0:32, :] = out[32 * p : 32 * p + 32, 0:128].astype(BF16)
        rest = [out[32 * p + 8 * i : 32 * p + 8 * i + 8, 128:256] for i in range(4)]
        packed = [jnp.where(left, rest[i], pltpu.roll(rest[3], 88 - 40 * i, 1)) for i in range(3)]
        out_ref[p, 32:56, :] = jnp.concatenate(packed, axis=0).astype(BF16)


def unpack_kernel(in_ref, out_hbm, out_ref, sems):
    out, inp = iota((128, 128), 0), iota((128, 128), 1)
    order = jnp.where(inp == ((out & 7) << 4) + (out >> 3), 1.0, 0.0).astype(BF16)
    lane = iota((128, 128), 1)
    left = lane < 72
    column = iota((8, 128), 1)
    rests = []
    for p in range(16):
        packed = in_ref[p, 32:56, :].astype(F32)
        h = [packed[8 * i : 8 * i + 8] for i in range(3)]
        last = jnp.where(column < 40, pltpu.roll(h[0], 40, 1), jnp.where(column < 80, pltpu.roll(h[1], 80, 1), pltpu.roll(h[2], 120, 1)))
        rests.append([jnp.concatenate(pair, axis=0).astype(BF16) for pair in ((h[0], h[1]), (h[2], last))])
    copies = []
    for b in range(2):
        halves = []
        for z in range(2):
            main = jnp.concatenate([in_ref[8 * z + e, 16 * b : 16 * b + 16, :] for e in range(8)], axis=0)
            rest = jnp.concatenate([rests[8 * z + e][b] for e in range(8)], axis=0)
            halves.append((dot(order, main), dot(order, rest)))
        (a0, a1), (b0, b1) = halves
        for c in range(3):
            if c == 0:
                upper = pltpu.roll(b0, 72, 1)
                first, second = jnp.where(left, a0, upper), upper
            elif c == 1:
                lower = jnp.where(lane < 56, pltpu.roll(a0, 56, 1), pltpu.roll(a1, 56, 1))
                first, second = jnp.where(left, lower, b0), b1
            else:
                upper = pltpu.roll(b1, 56, 1)
                first, second = jnp.where(left, pltpu.roll(a1, 112, 1), upper), upper
            rows = pl.ds(256 * c + 128 * b, 128)
            out_ref[rows, 0:128] = first.astype(BF16)
            out_ref[rows, 128:144] = second[:, 0:16].astype(BF16)
            copies.append(pltpu.make_async_copy(out_ref.at[rows], out_hbm.at[rows], sems.at[2 * c + b]))
            copies[-1].start()
    for copy in copies:
        copy.wait()


SMEM = pl.BlockSpec(memory_space=pltpu.SMEM)
VMEM = pl.BlockSpec(memory_space=pltpu.VMEM)
HBM = pl.BlockSpec(memory_space=pltpu.HBM)


def call(kernel, in_specs, out_shapes, scratch=(), aliases=None, out_specs=None):
    single = not isinstance(out_shapes, (list, tuple)) or hasattr(out_shapes, "shape")
    return pl.pallas_call(
        kernel,
        in_specs=in_specs,
        out_specs=out_specs or (VMEM if single else [VMEM] * len(out_shapes)),
        out_shape=out_shapes,
        scratch_shapes=list(scratch),
        compiler_params=pltpu.CompilerParams(vmem_limit_bytes=40 * 1024 * 1024),
        input_output_aliases=aliases or {},
        interpret=INTERPRET,
    )


def in_hbm(x):
    return x if INTERPRET else pltpu.with_memory_space_constraint(x, pltpu.HBM)


def shape(*dims):
    return jax.ShapeDtypeStruct(dims, BF16)


def on_device(velocity_modes, metric, face_partner, face_side, face_flip):
    blocks = lax.axis_size("elem")
    up = [(i, (i + 1) % blocks) for i in range(blocks)]
    down = [(j, i) for i, j in up]
    synth, analysis = fourier_tables(512, 768)
    pick, geometry = bf16(pick_table()), in_hbm(metric.T)
    send, own, to_prev, to_next, plan = call(
        functools.partial(pack_kernel, blocks),
        [HBM] * 7,
        [
            shape(2, 8, 144, 128),
            shape(192, 16, 128),
            shape(2, 8, 16, 128),
            shape(2, 8, 16, 128),
            jax.ShapeDtypeStruct((16, 128), jnp.int32),
        ],
        [
            pltpu.VMEM((4, 8), jnp.int32),
            pltpu.VMEM((4, 8), jnp.int32),
            pltpu.VMEM((4, 8), jnp.int32),
            pltpu.SMEM((4, 8), F32),
            pltpu.VMEM((768, 144), BF16),
            pltpu.VMEM((272, 144), BF16),
            pltpu.VMEM((80, 128), BF16),
            pltpu.VMEM((8, 128, 144), BF16),
            pltpu.VMEM((8, 16, 128), F32),
            pltpu.SMEM((16, 128), jnp.int32),
            pltpu.SemaphoreType.DMA((9,)),
        ],
        out_specs=[VMEM] * 5,
    )(
        in_hbm(face_partner.T),
        in_hbm(face_side.T),
        in_hbm(face_flip.T),
        geometry,
        in_hbm(velocity_modes.reshape(768, 144)),
        in_hbm(bf16(trace_table())),
        in_hbm(pick),
    )
    from_prev = lax.ppermute(to_next, "elem", up)
    from_next = lax.ppermute(to_prev, "elem", down)
    _, send = call(
        border_kernel,
        [VMEM] * 6,
        [shape(192, 16, 128), shape(2, 8, 144, 128)],
        [pltpu.SMEM((16, 128), jnp.int32), pltpu.SemaphoreType.DMA((1,))],
        aliases={4: 0, 5: 1},
    )(plan, from_prev, from_next, pick, own, send)
    got = lax.all_to_all(send.reshape(16, 144, 128), "plane", 0, 0, tiled=True)
    out = call(
        main_kernel,
        [HBM, VMEM, VMEM, VMEM, VMEM, VMEM],
        shape(16, 56, 128),
        [
            pltpu.VMEM((864, 512), BF16),
            pltpu.VMEM((256, 768), BF16),
            pltpu.SMEM((4, 8), F32),
            pltpu.SemaphoreType.DMA((1,)),
        ],
    )(geometry, got, bf16(point_table()), bf16(place_table()), bf16(synth), bf16(analysis))
    out = lax.all_to_all(out, "plane", 0, 0, tiled=True)
    out = call(
        unpack_kernel,
        [VMEM],
        shape(768, 144),
        [pltpu.VMEM((768, 144), BF16), pltpu.SemaphoreType.DMA((6,))],
        out_specs=HBM,
    )(out)
    return out.reshape(3, 32, 8, 144)


def solution(mesh):
    by_elem = P("elem", None)
    whole = P(None, "plane", "elem", None)
    return jax.shard_map(
        on_device,
        mesh=mesh,
        in_specs=(whole, by_elem, by_elem, by_elem, by_elem),
        out_specs=whole,
        check_vma=False,
    )
```

```python
import functools

import jax
import jax.numpy as jnp
import numpy as np
from jax import lax
from jax.experimental import pallas as pl
from jax.experimental.pallas import tpu as pltpu
from jax.sharding import PartitionSpec as P

F32, BF16 = jnp.float32, jnp.bfloat16
NT = (((1,), (1,)), ((), ()))
INTERPRET = False


def bf16(table):
    return jnp.asarray(np.asarray(table, np.float32)).astype(BF16)


def legendre_tables():
    points = -np.cos(np.pi * np.arange(12) / 11.0)
    values, slopes = np.zeros((12, 12)), np.zeros((12, 12))
    values[:, 0] = 1.0
    values[:, 1] = points
    slopes[:, 1] = 1.0
    for n in range(1, 11):
        values[:, n + 1] = ((2 * n + 1) * points * values[:, n] - n * values[:, n - 1]) / (n + 1)
        slopes[:, n + 1] = slopes[:, n - 1] + (2 * n + 1) * values[:, n]
    return np.kron(values, values), np.kron(slopes, values), np.kron(values, slopes)


def face_points(face):
    t = np.arange(12)
    return (t, 132 + t, 12 * t, 12 * t + 11)[face]


def trace_table():
    _, xi, eta = legendre_tables()
    table = np.zeros((272, 144))
    table[np.arange(16), 128 + np.arange(16)] = 1.0
    for face in range(4):
        q = face_points(face)
        for at, rows in ((16, xi[q]), (80, eta[q]), (144, xi[q[::-1]]), (208, eta[q[::-1]])):
            table[at + 16 * face : at + 16 * face + 12] = rows
    return table


def point_table():
    basis, xi, eta = legendre_tables()
    return np.stack([np.concatenate([t[72 * h : 72 * h + 72] for t in (basis, xi, eta)]) for h in range(2)])


def half_face_rows(h):
    own = [(h, t) for t in range(1, 11)]
    along = range(1, 6) if h == 0 else range(6, 11)
    return own + [(f, t) for f in (2, 3) for t in along]


def pick_table():
    table = np.zeros((80, 128))
    for h in range(2):
        for g in range(2):
            for i, (f, t) in enumerate(half_face_rows(h)):
                table[40 * h + 20 * g + i, 64 * g + 16 * f + t] = 1.0
    return table


def place_table():
    table = np.zeros((2, 144, 40))
    for h in range(2):
        for g in range(2):
            for i, (f, t) in enumerate(half_face_rows(h)):
                table[h, 72 * g + face_points(f)[t] - 72 * h, 20 * g + i] = 1.0
    return table


def fourier_tables(planes, phys):
    m = np.arange(planes) // 2
    odd = np.arange(planes) % 2 == 1
    theta = (2.0 * np.pi / phys) * ((np.arange(phys)[None, :] * m[:, None]) % phys)
    weight = np.where(m == 0, 1.0, 2.0)[:, None]
    synth = np.where(odd[:, None], -weight * np.sin(theta), weight * np.cos(theta))
    analysis = np.where(odd[:, None], -np.sin(theta), np.cos(theta)) / phys
    return synth, analysis


def iota(shape, axis):
    return lax.broadcasted_iota(jnp.int32, shape, axis)


def to_element_rows():
    out, inp = iota((128, 128), 0), iota((128, 128), 1)
    return jnp.where(inp == ((out & 15) << 3) + (out >> 4), 1.0, 0.0).astype(BF16)


def reverse_faces():
    out, inp = iota((128, 128), 0), iota((128, 128), 1)
    t = out & 15
    return jnp.where((t < 12) & (inp == out - t + 11 - t), 1.0, 0.0).astype(BF16)


def dot(a, b):
    return jnp.dot(a, b, preferred_element_type=F32)


def dot_nt(a, b):
    return lax.dot_general(a, b, NT, preferred_element_type=F32)


def dot_tn(a, b):
    return lax.dot_general(a, b, (((0,), (0,)), ((), ())), preferred_element_type=F32)


def neighbours(blocks):
    me = lax.axis_index("elem")
    step = 2 * lax.bitwise_and(me, 1) - 1
    return me, (lax.bitwise_and(me + step + blocks, blocks - 1), me - step)


def start_copies(pairs, sems):
    copies = [pltpu.make_async_copy(src, dst, sems.at[i]) for i, (src, dst) in enumerate(pairs)]
    for copy in copies:
        copy.start()
    return copies


def average(own_ref, pick, element, places):
    tiles = [None] * 8
    for f in range(4):
        for g in range(2):
            own = own_ref[16 * element + 4 * g + f].astype(F32)
            other = own_ref[places[f] + 4 * g].astype(F32)
            tiles[4 * g + f] = (0.5 * (own + other)).astype(BF16)
    return dot(pick, jnp.concatenate(tiles, axis=0))


def everywhere(reduce, x):
    return reduce(reduce(x, axis=1, keepdims=True), axis=0, keepdims=True)


def pack_kernel(
    blocks, partner_hbm, side_hbm, flip_hbm, metric_hbm, v_hbm, table_hbm, pick_hbm, send_ref, own_ref, first_ref, second_ref, plan_ref,
    partner_ref, side_ref, flip_ref, metric_ref, v_ref, table_ref, pick_ref, rows_ref, tail_ref, place_ref, sems,
):
    parts = [pl.ds(256 * i, 256) for i in range(3)]
    copies = start_copies(
        [(v_hbm.at[part], v_ref.at[part]) for part in parts]
        + [
            (table_hbm, table_ref),
            (partner_hbm, partner_ref),
            (metric_hbm, metric_ref),
            (side_hbm, side_ref),
            (flip_hbm, flip_ref),
            (pick_hbm, pick_ref),
        ],
        sems,
    )
    me, sides = neighbours(blocks)
    order = to_element_rows()
    rows_ref[:, 96:128, :] = jnp.zeros((8, 32, 144), BF16)
    for b in range(6):
        if b % 2 == 0:
            copies[b // 2].wait()
        block = dot(order, v_ref[128 * b : 128 * b + 128, :]).astype(BF16)
        for e in range(8):
            rows_ref[e, 16 * b : 16 * b + 16, :] = block[16 * e : 16 * e + 16]
    for copy in copies[3:]:
        copy.wait()
    p = partner_ref[...]
    home = p >> 3
    e, f = iota((4, 8), 1).astype(F32), iota((4, 8), 0).astype(F32)
    number = p.astype(F32)
    turn = (flip_ref[...] * 8 + side_ref[...]).astype(F32)
    there = [home == side for side in sides]
    low = [everywhere(jnp.min, jnp.where(t, e, 7.0)) for t in there]
    high = [everywhere(jnp.max, jnp.where(t, e, 0.0)) for t in there]
    least = [everywhere(jnp.min, jnp.where(t, number, 1e9)) for t in there]
    near = ((p & 7) << 4).astype(F32) + turn
    inside = jnp.where(home == me, near, 16.0 * e + f)
    first = jnp.where(number == least[0], 128.0, 144.0) + turn
    second = jnp.where(number == least[1], 160.0, 176.0) + turn
    plan_ref[0:4, 0:8] = inside.astype(jnp.int32)
    plan_ref[4:8, 0:8] = jnp.where(there[0], first, jnp.where(there[1], second, inside)).astype(jnp.int32)
    column = iota((1, 8), 1)
    ends = jnp.where(column == 0, low[0], jnp.where(column == 1, high[0], jnp.where(column == 2, low[1], high[1])))
    plan_ref[8:9, 0:8] = ends.astype(jnp.int32)
    (plan_copy,) = start_copies(((plan_ref, place_ref),), sems)
    table = table_ref[...]
    pick = pick_ref[...]
    for e in range(8):
        rows = rows_ref[e]
        out = dot_nt(table, rows)
        tail_ref[e] = out[0:16]
        for h in range(2):
            send_ref[h, e, 0:96, :] = rows[0:96, 0:128]
        for flip in range(2):
            xi = out[16 + 128 * flip : 80 + 128 * flip]
            eta = out[80 + 128 * flip : 144 + 128 * flip]
            for g in range(2):
                grad = xi * metric_ref[2 * g, e] + eta * metric_ref[2 * g + 1, e]
                at = 16 * e + 8 * flip + 4 * g
                own_ref[at : at + 4] = grad.astype(BF16).reshape(4, 16, 128)
    plan_copy.wait()
    taken = iota((40, 128), 1) < 96
    for i, out_ref in enumerate((first_ref, second_ref)):
        for k in range(2):
            out_ref[k] = own_ref[pl.ds(16 * place_ref[8, 2 * i + k], 8)]
    for e in range(8):
        out = average(own_ref, pick, e, [place_ref[f, e] for f in range(4)])
        upper = tail_ref[e, 8:16]
        spare = jnp.concatenate([pltpu.roll(upper, 96 - 32 * c, 1) for c in range(3)] + [jnp.zeros((16, 128), F32)], axis=0)
        for h in range(2):
            face = jnp.where(taken, out[40 * h : 40 * h + 40], spare)
            send_ref[h, e, 96:144, :] = jnp.concatenate([tail_ref[e, 0:8], face], axis=0).astype(BF16)


def border_kernel(plan_ref, first_ref, second_ref, pick_ref, own_in, send_in, own_ref, send_ref, place_ref, sems):
    (plan_copy,) = start_copies(((plan_ref, place_ref),), sems)
    reverse = reverse_faces()
    for k, ref in ((8, first_ref), (10, second_ref)):
        for i in range(2):
            at = 16 * (k + i)
            own_ref[at : at + 8] = ref[i]
            own_ref[at + 8 : at + 16] = dot(reverse, ref[i].reshape(128, 128)).astype(BF16).reshape(8, 16, 128)
    pick = pick_ref[...]
    row, lane = iota((48, 128), 0), iota((48, 128), 1)
    kept = (row < 8) | (lane >= 96)
    plan_copy.wait()
    for r in range(4):
        e = place_ref[8, r]
        out = average(own_ref, pick, e, [place_ref[4 + f, e] for f in range(4)])
        for h in range(2):
            old = send_ref[h, e, 96:144, :].astype(F32)
            face = jnp.concatenate([jnp.zeros((8, 128), F32), out[40 * h : 40 * h + 40]], axis=0)
            send_ref[h, e, 96:144, :] = jnp.where(kept, old, face).astype(BF16)


def regroup(blocks, lanes=(0, 32, 64)):
    rows = blocks[0].shape[0]
    lane = iota((rows, 128), 1) >> 5
    out = []
    for start in lanes:
        groups = []
        for first in range(0, len(blocks), 4):
            group = None
            for k in range(4):
                shift = (32 * k - start) % 128
                piece = pltpu.roll(blocks[first + k], shift, 1) if shift else blocks[first + k]
                group = piece if group is None else jnp.where(lane == k, piece, group)
            groups.append(group)
        out.append(jnp.concatenate(groups, axis=1))
    return out


def main_kernel(metric_hbm, got_ref, table_ref, place_ref, synth_ref, analysis_ref, out_ref, field_ref, adv_ref, metric_ref, sems):
    (copy,) = start_copies(((metric_hbm, metric_ref),), sems)
    position = lax.axis_index("plane")
    elem, half = lax.bitwise_and(position, 7), lax.shift_right_logical(position, 3)
    table = table_ref[half]
    place = place_ref[half]
    blocks = [got_ref[p, 96:144, :].astype(F32) for p in range(16)]
    lower = regroup([block[0:8] for block in blocks])
    upper = [regroup([block[8 * c + 8 : 8 * c + 16] for block in blocks], (96,))[0] for c in range(3)]
    tails = [jnp.concatenate([lower[c], upper[c]], axis=0) for c in range(3)]
    faces = regroup([block[8:48] for block in blocks])
    on_face = dot(place, jnp.ones((40, 128), BF16)) > 0.5
    lane = iota((72, 128), 1)
    even = (lane & 1) == 0
    copy.wait()
    m = [metric_ref[k, elem] for k in range(4)]
    for c in range(3):
        modes = jnp.concatenate([got_ref[p, 32 * c : 32 * c + 32, :] for p in range(16)], axis=0)
        d = dot_nt(table[:, 0:128], modes) + dot(table[:, 128:144], tails[c].astype(BF16))
        value = d[0:72].astype(BF16).astype(F32)
        xi, eta = d[72:144], d[144:216]
        turned = []
        for g in range(4):
            v = value[:, 128 * g : 128 * g + 128]
            k = ((lane + 128 * g) >> 1).astype(F32) * (1.0 / 32.0)
            turned.append(jnp.where(even, -k * pltpu.roll(v, 127, 1), k * pltpu.roll(v, 1, 1)))
        field_ref[288 * c : 288 * c + 144, :] = jnp.concatenate([value, jnp.concatenate(turned, axis=1)], axis=0).astype(BF16)
        grads = jnp.concatenate([xi * m[0] + eta * m[1], xi * m[2] + eta * m[3]], axis=0)
        at_faces = dot(place, faces[c].astype(BF16))
        grads = jnp.concatenate(
            [jnp.where(on_face, at_faces[:, at : at + 128], grads[:, at : at + 128]) for at in range(0, 512, 128)], axis=1
        )
        field_ref[288 * c + 144 : 288 * c + 288, :] = grads.astype(BF16)
    adv_ref[208:256, :] = jnp.zeros((48, 768), BF16)
    for j in range(0, 768, 256):
        phys = dot(field_ref[...], synth_ref[:, j : j + 256])
        terms = []
        for c in range(3):
            at = 288 * c
            terms.append(
                phys[0:72] * phys[at + 144 : at + 216]
                + phys[288:360] * phys[at + 216 : at + 288]
                + phys[576:648] * phys[at + 72 : at + 144]
            )
        terms.append(jnp.zeros((8, 256), F32))
        adv_ref[0:224, j : j + 256] = jnp.concatenate(terms, axis=0).astype(BF16)
    out = dot_nt(analysis_ref[...], adv_ref[...])
    left = iota((8, 128), 1) < 88
    for p in range(16):
        out_ref[p, 0:32, :] = out[32 * p : 32 * p + 32, 0:128].astype(BF16)
        rest = [out[32 * p + 8 * i : 32 * p + 8 * i + 8, 128:256] for i in range(4)]
        packed = [jnp.where(left, rest[i], pltpu.roll(rest[3], 88 - 40 * i, 1)) for i in range(3)]
        out_ref[p, 32:56, :] = jnp.concatenate(packed, axis=0).astype(BF16)


def unpack_kernel(in_ref, out_hbm, out_ref, sems):
    out, inp = iota((128, 128), 0), iota((128, 128), 1)
    order = jnp.where(inp == ((out & 7) << 4) + (out >> 3), 1.0, 0.0).astype(BF16)
    lane = iota((128, 128), 1)
    left = lane < 72
    column = iota((8, 128), 1)
    rests = []
    for p in range(16):
        packed = in_ref[p, 32:56, :].astype(F32)
        h = [packed[8 * i : 8 * i + 8] for i in range(3)]
        last = jnp.where(column < 40, pltpu.roll(h[0], 40, 1), jnp.where(column < 80, pltpu.roll(h[1], 80, 1), pltpu.roll(h[2], 120, 1)))
        rests.append([jnp.concatenate(pair, axis=0).astype(BF16) for pair in ((h[0], h[1]), (h[2], last))])
    copies = []
    for b in range(2):
        halves = []
        for z in range(2):
            main = jnp.concatenate([in_ref[8 * z + e, 16 * b : 16 * b + 16, :] for e in range(8)], axis=0)
            rest = jnp.concatenate([rests[8 * z + e][b] for e in range(8)], axis=0)
            halves.append((dot(order, main), dot(order, rest)))
        (a0, a1), (b0, b1) = halves
        for c in range(3):
            if c == 0:
                upper = pltpu.roll(b0, 72, 1)
                first, second = jnp.where(left, a0, upper), upper
            elif c == 1:
                lower = jnp.where(lane < 56, pltpu.roll(a0, 56, 1), pltpu.roll(a1, 56, 1))
                first, second = jnp.where(left, lower, b0), b1
            else:
                upper = pltpu.roll(b1, 56, 1)
                first, second = jnp.where(left, pltpu.roll(a1, 112, 1), upper), upper
            rows = pl.ds(256 * c + 128 * b, 128)
            out_ref[rows, 0:128] = first.astype(BF16)
            out_ref[rows, 128:144] = second[:, 0:16].astype(BF16)
            copies.append(pltpu.make_async_copy(out_ref.at[rows], out_hbm.at[rows], sems.at[2 * c + b]))
            copies[-1].start()
    for copy in copies:
        copy.wait()


SMEM = pl.BlockSpec(memory_space=pltpu.SMEM)
VMEM = pl.BlockSpec(memory_space=pltpu.VMEM)
HBM = pl.BlockSpec(memory_space=pltpu.HBM)


def call(kernel, in_specs, out_shapes, scratch=(), aliases=None, out_specs=None):
    single = not isinstance(out_shapes, (list, tuple)) or hasattr(out_shapes, "shape")
    return pl.pallas_call(
        kernel,
        in_specs=in_specs,
        out_specs=out_specs or (VMEM if single else [VMEM] * len(out_shapes)),
        out_shape=out_shapes,
        scratch_shapes=list(scratch),
        compiler_params=pltpu.CompilerParams(vmem_limit_bytes=40 * 1024 * 1024),
        input_output_aliases=aliases or {},
        interpret=INTERPRET,
    )


def in_hbm(x):
    return x if INTERPRET else pltpu.with_memory_space_constraint(x, pltpu.HBM)


def shape(*dims):
    return jax.ShapeDtypeStruct(dims, BF16)


def on_device(velocity_modes, metric, face_partner, face_side, face_flip):
    blocks = lax.axis_size("elem")
    across = [((i + 1) % blocks, ((i ^ 1) + 1) % blocks) for i in range(blocks)]
    within = [(i, i ^ 1) for i in range(blocks)]
    synth, analysis = fourier_tables(512, 768)
    pick, geometry = bf16(pick_table()), in_hbm(metric.T)
    send, own, to_first, to_second, plan = call(
        functools.partial(pack_kernel, blocks),
        [HBM] * 7,
        [
            shape(2, 8, 144, 128),
            shape(192, 16, 128),
            shape(2, 8, 16, 128),
            shape(2, 8, 16, 128),
            jax.ShapeDtypeStruct((16, 128), jnp.int32),
        ],
        [
            pltpu.VMEM((4, 8), jnp.int32),
            pltpu.VMEM((4, 8), jnp.int32),
            pltpu.VMEM((4, 8), jnp.int32),
            pltpu.SMEM((4, 8), F32),
            pltpu.VMEM((768, 144), BF16),
            pltpu.VMEM((272, 144), BF16),
            pltpu.VMEM((80, 128), BF16),
            pltpu.VMEM((8, 128, 144), BF16),
            pltpu.VMEM((8, 16, 128), F32),
            pltpu.SMEM((16, 128), jnp.int32),
            pltpu.SemaphoreType.DMA((9,)),
        ],
        out_specs=[VMEM] * 5,
    )(
        in_hbm(face_partner.T),
        in_hbm(face_side.T),
        in_hbm(face_flip.T),
        geometry,
        in_hbm(velocity_modes.reshape(768, 144)),
        in_hbm(bf16(trace_table())),
        in_hbm(pick),
    )
    from_first = lax.ppermute(to_first, "elem", across)
    from_second = lax.ppermute(to_second, "elem", within)
    _, send = call(
        border_kernel,
        [VMEM] * 6,
        [shape(192, 16, 128), shape(2, 8, 144, 128)],
        [pltpu.SMEM((16, 128), jnp.int32), pltpu.SemaphoreType.DMA((1,))],
        aliases={4: 0, 5: 1},
    )(plan, from_first, from_second, pick, own, send)
    got = lax.all_to_all(send.reshape(16, 144, 128), "plane", 0, 0, tiled=True)
    out = call(
        main_kernel,
        [HBM, VMEM, VMEM, VMEM, VMEM, VMEM],
        shape(16, 56, 128),
        [
            pltpu.VMEM((864, 512), BF16),
            pltpu.VMEM((256, 768), BF16),
            pltpu.SMEM((4, 8), F32),
            pltpu.SemaphoreType.DMA((1,)),
        ],
    )(geometry, got, bf16(point_table()), bf16(place_table()), bf16(synth), bf16(analysis))
    out = lax.all_to_all(out, "plane", 0, 0, tiled=True)
    out = call(
        unpack_kernel,
        [VMEM],
        shape(768, 144),
        [pltpu.VMEM((768, 144), BF16), pltpu.SemaphoreType.DMA((6,))],
        out_specs=HBM,
    )(out)
    return out.reshape(3, 32, 8, 144)


def solution(mesh):
    by_elem = P("elem", None)
    whole = P(None, "plane", "elem", None)
    return jax.shard_map(
        on_device,
        mesh=mesh,
        in_specs=(whole, by_elem, by_elem, by_elem, by_elem),
        out_specs=whole,
        check_vma=False,
    )
```

```python
import functools

import jax
import jax.numpy as jnp
import numpy as np
from jax import lax
from jax.experimental import pallas as pl
from jax.experimental.pallas import tpu as pltpu
from jax.sharding import PartitionSpec as P

F32, BF16 = jnp.float32, jnp.bfloat16
NT = (((1,), (1,)), ((), ()))
INTERPRET = False


def bf16(table):
    return jnp.asarray(np.asarray(table, np.float32)).astype(BF16)


def legendre_tables():
    points = -np.cos(np.pi * np.arange(12) / 11.0)
    values, slopes = np.zeros((12, 12)), np.zeros((12, 12))
    values[:, 0] = 1.0
    values[:, 1] = points
    slopes[:, 1] = 1.0
    for n in range(1, 11):
        values[:, n + 1] = ((2 * n + 1) * points * values[:, n] - n * values[:, n - 1]) / (n + 1)
        slopes[:, n + 1] = slopes[:, n - 1] + (2 * n + 1) * values[:, n]
    return np.kron(values, values), np.kron(slopes, values), np.kron(values, slopes)


def face_points(face):
    t = np.arange(12)
    return (t, 132 + t, 12 * t, 12 * t + 11)[face]


def trace_table():
    _, xi, eta = legendre_tables()
    table = np.zeros((144, 144))
    table[np.arange(16), 128 + np.arange(16)] = 1.0
    for face in range(4):
        q = face_points(face)
        for at, rows in ((16, xi[q]), (80, eta[q])):
            table[at + 16 * face : at + 16 * face + 12] = rows
    return table


def point_table():
    basis, xi, eta = legendre_tables()
    return np.stack([np.concatenate([t[72 * h : 72 * h + 72] for t in (basis, xi, eta)]) for h in range(2)])


def half_face_rows(h):
    own = [(h, t) for t in range(1, 11)]
    along = range(1, 6) if h == 0 else range(6, 11)
    return own + [(f, t) for f in (2, 3) for t in along]


def pick_table():
    table = np.zeros((80, 128))
    for h in range(2):
        for g in range(2):
            for i, (f, t) in enumerate(half_face_rows(h)):
                table[40 * h + 20 * g + i, 64 * g + 16 * f + t] = 1.0
    return table


def place_table():
    table = np.zeros((2, 144, 40))
    for h in range(2):
        for g in range(2):
            for i, (f, t) in enumerate(half_face_rows(h)):
                table[h, 72 * g + face_points(f)[t] - 72 * h, 20 * g + i] = 1.0
    return table


def fourier_tables(planes, phys):
    m = np.arange(planes) // 2
    odd = np.arange(planes) % 2 == 1
    theta = (2.0 * np.pi / phys) * ((np.arange(phys)[None, :] * m[:, None]) % phys)
    weight = np.where(m == 0, 1.0, 2.0)[:, None]
    synth = np.where(odd[:, None], -weight * np.sin(theta), weight * np.cos(theta))
    analysis = np.where(odd[:, None], -np.sin(theta), np.cos(theta)) / phys
    return synth, analysis


def iota(shape, axis):
    return lax.broadcasted_iota(jnp.int32, shape, axis)


def to_element_rows():
    out, inp = iota((128, 128), 0), iota((128, 128), 1)
    return jnp.where(inp == ((out & 15) << 3) + (out >> 4), 1.0, 0.0).astype(BF16)


def reverse_faces():
    out, inp = iota((128, 128), 0), iota((128, 128), 1)
    t = out & 15
    return jnp.where((t < 12) & (inp == out - t + 11 - t), 1.0, 0.0).astype(BF16)


def dot(a, b):
    return jnp.dot(a, b, preferred_element_type=F32)


def dot_nt(a, b):
    return lax.dot_general(a, b, NT, preferred_element_type=F32)


def dot_tn(a, b):
    return lax.dot_general(a, b, (((0,), (0,)), ((), ())), preferred_element_type=F32)


def neighbours(blocks):
    me = lax.axis_index("elem")
    return me, (lax.bitwise_and(me + blocks - 1, blocks - 1), lax.bitwise_and(me + 1, blocks - 1))


def start_copies(pairs, sems):
    copies = [pltpu.make_async_copy(src, dst, sems.at[i]) for i, (src, dst) in enumerate(pairs)]
    for copy in copies:
        copy.start()
    return copies


def average(own_ref, pick, element, places):
    tiles = [None] * 8
    for f in range(4):
        for g in range(2):
            own = own_ref[16 * element + 4 * g + f].astype(F32)
            other = own_ref[places[f] + 4 * g].astype(F32)
            tiles[4 * g + f] = (0.5 * (own + other)).astype(BF16)
    return dot(pick, jnp.concatenate(tiles, axis=0))


def everywhere(reduce, x):
    return reduce(reduce(x, axis=1, keepdims=True), axis=0, keepdims=True)


def trace_kernel(
    blocks, partner_hbm, side_hbm, flip_hbm, metric_hbm, v_hbm, table_hbm, rows_ref, tail_ref, own_ref, prev_ref, next_ref, plan_ref,
    partner_ref, side_ref, flip_ref, metric_ref, v_ref, table_ref, place_ref, sems,
):
    parts = [pl.ds(256 * i, 256) for i in range(3)]
    copies = start_copies(
        [(v_hbm.at[part], v_ref.at[part]) for part in parts]
        + [
            (table_hbm, table_ref),
            (partner_hbm, partner_ref),
            (metric_hbm, metric_ref),
            (side_hbm, side_ref),
            (flip_hbm, flip_ref),
        ],
        sems,
    )
    me, sides = neighbours(blocks)
    order = to_element_rows()
    rows_ref[:, 96:128, :] = jnp.zeros((8, 32, 144), BF16)
    for b in range(6):
        if b % 2 == 0:
            copies[b // 2].wait()
        block = dot(order, v_ref[128 * b : 128 * b + 128, :]).astype(BF16)
        for e in range(8):
            rows_ref[e, 16 * b : 16 * b + 16, :] = block[16 * e : 16 * e + 16]
    for copy in copies[3:]:
        copy.wait()
    p = partner_ref[...]
    home = p >> 3
    e, f = iota((4, 8), 1).astype(F32), iota((4, 8), 0).astype(F32)
    number = p.astype(F32)
    turn = (flip_ref[...] * 8 + side_ref[...]).astype(F32)
    there = [home == side for side in sides]
    low = [everywhere(jnp.min, jnp.where(t, e, 7.0)) for t in there]
    high = [everywhere(jnp.max, jnp.where(t, e, 0.0)) for t in there]
    least = [everywhere(jnp.min, jnp.where(t, number, 1e9)) for t in there]
    near = ((p & 7) << 4).astype(F32) + turn
    inside = jnp.where(home == me, near, 16.0 * e + f)
    first = jnp.where(number == least[0], 128.0, 144.0) + turn
    second = jnp.where(number == least[1], 160.0, 176.0) + turn
    plan_ref[0:4, 0:8] = inside.astype(jnp.int32)
    plan_ref[4:8, 0:8] = jnp.where(there[0], first, jnp.where(there[1], second, inside)).astype(jnp.int32)
    column = iota((1, 8), 1)
    ends = jnp.where(column == 0, low[0], jnp.where(column == 1, high[0], jnp.where(column == 2, low[1], high[1])))
    plan_ref[8:9, 0:8] = ends.astype(jnp.int32)
    (plan_copy,) = start_copies(((plan_ref, place_ref),), sems)
    table = table_ref[...]
    for e in range(8):
        out = dot_nt(table, rows_ref[e])
        tail_ref[e] = out[0:16]
        xi, eta = out[16:80], out[80:144]
        for g in range(2):
            grad = xi * metric_ref[2 * g, e] + eta * metric_ref[2 * g + 1, e]
            at = 16 * e + 4 * g
            own_ref[at : at + 4] = grad.astype(BF16).reshape(4, 16, 128)
    plan_copy.wait()
    for i, out_ref in enumerate((prev_ref, next_ref)):
        for k in range(2):
            out_ref[k] = own_ref[pl.ds(16 * place_ref[8, 2 * i + k], 8)]


def pack_kernel(plan_ref, rows_ref, tail_ref, own_in, pick_ref, send_ref, own_ref, place_ref, sems):
    (plan_copy,) = start_copies(((plan_ref, place_ref),), sems)
    pick = pick_ref[...]
    taken = iota((40, 128), 1) < 96
    reverse = reverse_faces()
    for e in range(8):
        forward = own_ref[16 * e : 16 * e + 8].reshape(128, 128)
        own_ref[16 * e + 8 : 16 * e + 16] = dot(reverse, forward).astype(BF16).reshape(8, 16, 128)
        rows = rows_ref[e, 0:96, 0:128]
        for h in range(2):
            send_ref[h, e, 0:96, :] = rows
    plan_copy.wait()
    for e in range(8):
        out = average(own_ref, pick, e, [place_ref[f, e] for f in range(4)])
        upper = tail_ref[e, 8:16]
        spare = jnp.concatenate([pltpu.roll(upper, 96 - 32 * c, 1) for c in range(3)] + [jnp.zeros((16, 128), F32)], axis=0)
        for h in range(2):
            face = jnp.where(taken, out[40 * h : 40 * h + 40], spare)
            send_ref[h, e, 96:144, :] = jnp.concatenate([tail_ref[e, 0:8], face], axis=0).astype(BF16)


def border_kernel(plan_ref, prev_ref, next_ref, pick_ref, own_in, send_in, own_ref, send_ref, place_ref, sems):
    (plan_copy,) = start_copies(((plan_ref, place_ref),), sems)
    reverse = reverse_faces()
    for k, ref in ((8, prev_ref), (10, next_ref)):
        for i in range(2):
            at = 16 * (k + i)
            own_ref[at : at + 8] = ref[i]
            own_ref[at + 8 : at + 16] = dot(reverse, ref[i].reshape(128, 128)).astype(BF16).reshape(8, 16, 128)
    pick = pick_ref[...]
    row, lane = iota((48, 128), 0), iota((48, 128), 1)
    kept = (row < 8) | (lane >= 96)
    plan_copy.wait()
    for r in range(4):
        e = place_ref[8, r]
        out = average(own_ref, pick, e, [place_ref[4 + f, e] for f in range(4)])
        for h in range(2):
            old = send_ref[h, e, 96:144, :].astype(F32)
            face = jnp.concatenate([jnp.zeros((8, 128), F32), out[40 * h : 40 * h + 40]], axis=0)
            send_ref[h, e, 96:144, :] = jnp.where(kept, old, face).astype(BF16)


def regroup(blocks, lanes=(0, 32, 64)):
    rows = blocks[0].shape[0]
    lane = iota((rows, 128), 1) >> 5
    out = []
    for start in lanes:
        groups = []
        for first in range(0, len(blocks), 4):
            group = None
            for k in range(4):
                shift = (32 * k - start) % 128
                piece = pltpu.roll(blocks[first + k], shift, 1) if shift else blocks[first + k]
                group = piece if group is None else jnp.where(lane == k, piece, group)
            groups.append(group)
        out.append(jnp.concatenate(groups, axis=1))
    return out


def main_kernel(metric_hbm, got_ref, table_ref, place_ref, synth_ref, analysis_ref, out_ref, field_ref, adv_ref, metric_ref, sems):
    (copy,) = start_copies(((metric_hbm, metric_ref),), sems)
    position = lax.axis_index("plane")
    elem, half = lax.bitwise_and(position, 7), lax.shift_right_logical(position, 3)
    table = table_ref[half]
    place = place_ref[half]
    blocks = [got_ref[p, 96:144, :].astype(F32) for p in range(16)]
    lower = regroup([block[0:8] for block in blocks])
    upper = [regroup([block[8 * c + 8 : 8 * c + 16] for block in blocks], (96,))[0] for c in range(3)]
    tails = [jnp.concatenate([lower[c], upper[c]], axis=0) for c in range(3)]
    faces = regroup([block[8:48] for block in blocks])
    on_face = dot(place, jnp.ones((40, 128), BF16)) > 0.5
    lane = iota((72, 128), 1)
    even = (lane & 1) == 0
    copy.wait()
    m = [metric_ref[k, elem] for k in range(4)]
    for c in range(3):
        modes = jnp.concatenate([got_ref[p, 32 * c : 32 * c + 32, :] for p in range(16)], axis=0)
        d = dot_nt(table[:, 0:128], modes) + dot(table[:, 128:144], tails[c].astype(BF16))
        value = d[0:72].astype(BF16).astype(F32)
        xi, eta = d[72:144], d[144:216]
        turned = []
        for g in range(4):
            v = value[:, 128 * g : 128 * g + 128]
            k = ((lane + 128 * g) >> 1).astype(F32) * (1.0 / 32.0)
            turned.append(jnp.where(even, -k * pltpu.roll(v, 127, 1), k * pltpu.roll(v, 1, 1)))
        field_ref[288 * c : 288 * c + 144, :] = jnp.concatenate([value, jnp.concatenate(turned, axis=1)], axis=0).astype(BF16)
        grads = jnp.concatenate([xi * m[0] + eta * m[1], xi * m[2] + eta * m[3]], axis=0)
        at_faces = dot(place, faces[c].astype(BF16))
        grads = jnp.concatenate(
            [jnp.where(on_face, at_faces[:, at : at + 128], grads[:, at : at + 128]) for at in range(0, 512, 128)], axis=1
        )
        field_ref[288 * c + 144 : 288 * c + 288, :] = grads.astype(BF16)
    adv_ref[208:256, :] = jnp.zeros((48, 768), BF16)
    for j in range(0, 768, 256):
        phys = dot(field_ref[...], synth_ref[:, j : j + 256])
        terms = []
        for c in range(3):
            at = 288 * c
            terms.append(
                phys[0:72] * phys[at + 144 : at + 216]
                + phys[288:360] * phys[at + 216 : at + 288]
                + phys[576:648] * phys[at + 72 : at + 144]
            )
        terms.append(jnp.zeros((8, 256), F32))
        adv_ref[0:224, j : j + 256] = jnp.concatenate(terms, axis=0).astype(BF16)
    out = dot_nt(analysis_ref[...], adv_ref[...])
    left = iota((8, 128), 1) < 88
    for p in range(16):
        out_ref[p, 0:32, :] = out[32 * p : 32 * p + 32, 0:128].astype(BF16)
        rest = [out[32 * p + 8 * i : 32 * p + 8 * i + 8, 128:256] for i in range(4)]
        packed = [jnp.where(left, rest[i], pltpu.roll(rest[3], 88 - 40 * i, 1)) for i in range(3)]
        out_ref[p, 32:56, :] = jnp.concatenate(packed, axis=0).astype(BF16)


def unpack_kernel(in_ref, out_hbm, out_ref, sems):
    out, inp = iota((128, 128), 0), iota((128, 128), 1)
    order = jnp.where(inp == ((out & 7) << 4) + (out >> 3), 1.0, 0.0).astype(BF16)
    lane = iota((128, 128), 1)
    left = lane < 72
    column = iota((8, 128), 1)
    rests = []
    for p in range(16):
        packed = in_ref[p, 32:56, :].astype(F32)
        h = [packed[8 * i : 8 * i + 8] for i in range(3)]
        last = jnp.where(column < 40, pltpu.roll(h[0], 40, 1), jnp.where(column < 80, pltpu.roll(h[1], 80, 1), pltpu.roll(h[2], 120, 1)))
        rests.append([jnp.concatenate(pair, axis=0).astype(BF16) for pair in ((h[0], h[1]), (h[2], last))])
    copies = []
    for b in range(2):
        halves = []
        for z in range(2):
            main = jnp.concatenate([in_ref[8 * z + e, 16 * b : 16 * b + 16, :] for e in range(8)], axis=0)
            rest = jnp.concatenate([rests[8 * z + e][b] for e in range(8)], axis=0)
            halves.append((dot(order, main), dot(order, rest)))
        (a0, a1), (b0, b1) = halves
        for c in range(3):
            if c == 0:
                upper = pltpu.roll(b0, 72, 1)
                first, second = jnp.where(left, a0, upper), upper
            elif c == 1:
                lower = jnp.where(lane < 56, pltpu.roll(a0, 56, 1), pltpu.roll(a1, 56, 1))
                first, second = jnp.where(left, lower, b0), b1
            else:
                upper = pltpu.roll(b1, 56, 1)
                first, second = jnp.where(left, pltpu.roll(a1, 112, 1), upper), upper
            rows = pl.ds(256 * c + 128 * b, 128)
            out_ref[rows, 0:128] = first.astype(BF16)
            out_ref[rows, 128:144] = second[:, 0:16].astype(BF16)
            copies.append(pltpu.make_async_copy(out_ref.at[rows], out_hbm.at[rows], sems.at[2 * c + b]))
            copies[-1].start()
    for copy in copies:
        copy.wait()


SMEM = pl.BlockSpec(memory_space=pltpu.SMEM)
VMEM = pl.BlockSpec(memory_space=pltpu.VMEM)
HBM = pl.BlockSpec(memory_space=pltpu.HBM)


def call(kernel, in_specs, out_shapes, scratch=(), aliases=None, out_specs=None):
    single = not isinstance(out_shapes, (list, tuple)) or hasattr(out_shapes, "shape")
    return pl.pallas_call(
        kernel,
        in_specs=in_specs,
        out_specs=out_specs or (VMEM if single else [VMEM] * len(out_shapes)),
        out_shape=out_shapes,
        scratch_shapes=list(scratch),
        compiler_params=pltpu.CompilerParams(vmem_limit_bytes=40 * 1024 * 1024),
        input_output_aliases=aliases or {},
        interpret=INTERPRET,
    )


def in_hbm(x):
    return x if INTERPRET else pltpu.with_memory_space_constraint(x, pltpu.HBM)


def shape(*dims):
    return jax.ShapeDtypeStruct(dims, BF16)


def on_device(velocity_modes, metric, face_partner, face_side, face_flip):
    blocks = lax.axis_size("elem")
    up = [(i, (i + 1) % blocks) for i in range(blocks)]
    down = [(j, i) for i, j in up]
    synth, analysis = fourier_tables(512, 768)
    pick, geometry = bf16(pick_table()), in_hbm(metric.T)
    plan_shape = jax.ShapeDtypeStruct((16, 128), jnp.int32)
    small = pltpu.VMEM((4, 8), jnp.int32)
    rows, tail, own, to_prev, to_next, plan = call(
        functools.partial(trace_kernel, blocks),
        [HBM] * 6,
        [
            shape(8, 128, 144),
            jax.ShapeDtypeStruct((8, 16, 128), F32),
            shape(192, 16, 128),
            shape(2, 8, 16, 128),
            shape(2, 8, 16, 128),
            plan_shape,
        ],
        [
            small,
            small,
            small,
            pltpu.SMEM((4, 8), F32),
            pltpu.VMEM((768, 144), BF16),
            pltpu.VMEM((144, 144), BF16),
            pltpu.SMEM((16, 128), jnp.int32),
            pltpu.SemaphoreType.DMA((8,)),
        ],
    )(
        in_hbm(face_partner.T),
        in_hbm(face_side.T),
        in_hbm(face_flip.T),
        geometry,
        in_hbm(velocity_modes.reshape(768, 144)),
        in_hbm(bf16(trace_table())),
    )
    from_prev = lax.ppermute(to_next, "elem", up)
    from_next = lax.ppermute(to_prev, "elem", down)
    send, own = call(
        pack_kernel,
        [VMEM] * 5,
        [shape(2, 8, 144, 128), shape(192, 16, 128)],
        [pltpu.SMEM((16, 128), jnp.int32), pltpu.SemaphoreType.DMA((1,))],
        aliases={3: 1},
    )(plan, rows, tail, own, pick)
    _, send = call(
        border_kernel,
        [VMEM] * 6,
        [shape(192, 16, 128), shape(2, 8, 144, 128)],
        [pltpu.SMEM((16, 128), jnp.int32), pltpu.SemaphoreType.DMA((1,))],
        aliases={4: 0, 5: 1},
    )(plan, from_prev, from_next, pick, own, send)
    got = lax.all_to_all(send.reshape(16, 144, 128), "plane", 0, 0, tiled=True)
    out = call(
        main_kernel,
        [HBM, VMEM, VMEM, VMEM, VMEM, VMEM],
        shape(16, 56, 128),
        [
            pltpu.VMEM((864, 512), BF16),
            pltpu.VMEM((256, 768), BF16),
            pltpu.SMEM((4, 8), F32),
            pltpu.SemaphoreType.DMA((1,)),
        ],
    )(geometry, got, bf16(point_table()), bf16(place_table()), bf16(synth), bf16(analysis))
    out = lax.all_to_all(out, "plane", 0, 0, tiled=True)
    out = call(
        unpack_kernel,
        [VMEM],
        shape(768, 144),
        [pltpu.VMEM((768, 144), BF16), pltpu.SemaphoreType.DMA((6,))],
        out_specs=HBM,
    )(out)
    return out.reshape(3, 32, 8, 144)


def solution(mesh):
    by_elem = P("elem", None)
    whole = P(None, "plane", "elem", None)
    return jax.shard_map(
        on_device,
        mesh=mesh,
        in_specs=(whole, by_elem, by_elem, by_elem, by_elem),
        out_specs=whole,
        check_vma=False,
    )
```
